32 devices in a mesh: lon: 8 (over y, x, core), bal: 4 (over z).
Axes of the slice: x: 2, y: 2, z: 4, core: 2. Of those that a mesh axis runs over, the one named last changes fastest.
Arguments:
- conc: float32 [65536, 128], P(('lon', 'bal')), may hold values from -6 to 6
- neighbours: int32 [512, 8], P(('lon', 'bal')), may hold values from 0 to 511, as said below
- counts: int32 [512], P(('lon', 'bal')), may hold values from 1 to 8
- weights: int32 [512, 8], P(('lon', 'bal')), may hold values from 1 to 15
- zones: int32 [65536], P(('lon', 'bal')), may hold values from 0 to 31
- owners: int32 [65536, 1], P(('lon', 'bal')), may hold values from 0 to 3; in each aligned block of 2048 rows (0 to 2047, 2048 to 4095, ...) at most 1024 rows name the same one
- rate_table: float32 [32, 128], replicated, may hold values from 0.05 to 1
- reaction: bfloat16 [128, 128], replicated, may hold values from -0.5 to 0.5
Outputs:
- conc_out: bfloat16 [65536, 128], P(('lon', 'bal'))
- chem_slots: bfloat16 [131072, 128], P(('lon', 'bal'))
The draws below stay inside these ranges and needn't reach their ends.
Inputs may be any that keep to these rules, and one draw needn't show every extreme that they name: neighbours[g, k] is a block of the same bal index as g, on the same longitude band or on the band just before or after it, with the bands wrapping around. On every trajectory owner, at most 1024 of its parcels have the same owners value; on some trajectory owners one value is taken exactly 1024 times.
All inputs are finite; a program needn't handle non-finite values.
Results may differ from the reference program's by a relative error of at most 0.0085.
Values may be sent and summed in bfloat16 or wider, within the bound.
No kernel may reach another device: no remote copies, remote signals or barrier semaphores. Data moves between devices by JAX's collectives and lax.ppermute only.
A program may use at most 64 MiB of HBM per device.

```python
import math
import jax
import jax.numpy as jnp
import numpy as np
from jax import lax

S = 128
BLK = 128
KADJ = 8
ZONES = 32
SUBSTEPS = 12
NB_DEV = 16
P_DEV = 2048
PARCELS = 65536
NBLOCKS = 512
BAND = 64
CAP = 1024
SLOTS = 131072
N_LON = 8
N_BAL = 4


def draw_neighbours(key, part):
    key_side, key_local = jax.random.split(jax.random.fold_in(key, 17))
    side = jax.random.randint(key_side, (NBLOCKS, KADJ), -1, 2, dtype=jnp.int32)
    local = jax.random.randint(key_local, (NBLOCKS, KADJ), 0, NB_DEV, dtype=jnp.int32)
    block = jnp.arange(NBLOCKS, dtype=jnp.int32)[:, None]
    first = block // NB_DEV * NB_DEV
    return ((first + side * BAND + local + NBLOCKS) % NBLOCKS).astype(jnp.int32)


def set_ends(result, key, least, high):
    shape = result.shape
    place = [jax.random.randint(jax.random.fold_in(key, axis), (), 0, shape[axis]) for axis in range(len(shape))]
    result = result.at[tuple(place)].set(least)
    longest = shape.index(max(shape))
    place[longest] = (place[longest] + 1) % shape[longest]
    return result.at[tuple(place)].set(high)


def levels(own_key, dims, shards, smallest, top_value):
    def one(dim, blocks):
        draws = jax.random.uniform(jax.random.fold_in(jax.random.fold_in(own_key, 6), dim), (blocks,), jnp.float32, smallest / len(shards), top_value / len(shards))
        return jnp.repeat(jnp.exp(draws), dims[dim] // blocks).reshape((-1,) + (1,) * (len(dims) - dim - 1))

    gain = one(*shards[0])
    for cut in shards[1:]:
        gain = gain * one(*cut)
    return gain


def shared_out(stream_key, own, number, rows, number_of, top, limit, lean):
    ranking = jax.random.permutation(stream_key, number_of)
    heavy_load, usual = shares(number_of, rows * top, limit, lean, True), shares(number_of, rows * top, limit, lean, False)
    places = jnp.arange(number_of)

    def named(tallies, turn):
        used = int((tallies > 0).sum())
        fixed = max(1, used // 4)
        moved = fixed + (places - fixed + turn * (used - fixed)) % max(1, number_of - fixed)
        return jnp.zeros((number_of,), jnp.int32).at[ranking[jnp.where(places < fixed, places, moved)]].set(jnp.asarray(tallies, jnp.int32))

    tallies = jnp.where(number % 4 == 0, named(heavy_load, number // 4), named(usual, number - number // 4 - 1))
    mixed = jax.random.permutation(jax.random.fold_in(own, 3), number_of)
    donor, sink = mixed[0:number_of // 2 * 2:2], mixed[1:number_of // 2 * 2:2]
    slack = jnp.minimum(tallies[donor] - 1, limit - tallies[sink]) // 2
    slack = jnp.where((donor == ranking[0]) | (sink == ranking[0]) | (tallies[sink] == 0), 0, jnp.maximum(slack, 0))
    moved = jax.random.randint(jax.random.fold_in(own, 4), (number_of // 2,), 0, 1 << 20) % (slack + 1)
    tallies = tallies.at[donor].add(-moved).at[sink].add(moved)
    labels = jnp.searchsorted(jnp.cumsum(tallies), jnp.arange(rows * top), side="right").astype(jnp.int32)
    table = labels.reshape(top, rows).T
    table = table[jax.random.permutation(jax.random.fold_in(own, 1), rows)]
    turn = jax.random.randint(jax.random.fold_in(own, 2), (rows, 1), 0, top)
    return jnp.take_along_axis(table, (jnp.arange(top)[None, :] + turn) % top, axis=1)


def shares(count, total, limit, slope, full):
    loads = [(1 << 20) // math.isqrt(rank ** slope) + 1 for rank in range(1, count + 1)]
    largest = limit if full else min(limit, max(-(-total // count), total * loads[0] // sum(loads)))
    least = 1 if total - largest >= count - 1 else 0
    given, surplus = [largest] + [least] * (count - 1), total - largest - least * (count - 1)
    while surplus > 0:
        movable = [i for i in range(1, count) if given[i] < largest] or [i for i in range(1, count) if given[i] < limit]
        mass, remaining = sum([loads[i] for i in movable]), surplus
        for i in movable:
            more = min(limit - given[i], max(1, remaining * loads[i] // mass), surplus)
            given[i] = given[i] + more
            surplus = surplus - more
    return np.array(given)


def gaussian(key, dims, deviation, most, pieces=(), kind=jnp.bfloat16):
    drawn = deviation * jax.random.normal(key, dims, jnp.float32)
    if pieces:
        drawn = drawn * levels(key, dims, pieces, -0.22, 0.18)
    return jnp.clip(drawn, -most, most).astype(kind)


def setup_inputs(seed: int = 0) -> dict:
    key_list = jax.random.split(jax.random.key(seed), 9)
    conc = gaussian(key_list[0], (PARCELS, S), 1.0, 6.0, ((0, 32),), jnp.float32)
    neighbours = draw_neighbours(jax.random.fold_in(key_list[8], 71), 0)
    counts = set_ends(jax.random.randint(key_list[2], (NBLOCKS,), 1, KADJ + 1), jax.random.fold_in(key_list[2], 1), 1, KADJ).astype(jnp.int32)
    weights = set_ends(jax.random.randint(key_list[3], (NBLOCKS, KADJ), 1, 16), jax.random.fold_in(key_list[3], 1), 1, 15).astype(jnp.int32)
    zones = set_ends(jax.random.randint(key_list[4], (PARCELS,), 0, ZONES), jax.random.fold_in(key_list[4], 1), 0, ZONES - 1).astype(jnp.int32)
    owners_keys = jax.random.split(jax.random.fold_in(key_list[5], 1), PARCELS // P_DEV)
    owners_turns = jax.random.permutation(jax.random.fold_in(key_list[5], 3), PARCELS // P_DEV)
    owners = jax.vmap(lambda own, number: shared_out(jax.random.fold_in(key_list[5], 2), own, number, P_DEV, N_BAL, 1, CAP, 1))(owners_keys, owners_turns).reshape((PARCELS, 1))
    rate_table = jnp.clip(jnp.exp(jax.random.uniform(key_list[6], (ZONES, S), jnp.float32, math.log(0.05), math.log(1.0))), 0.05, 1.0)
    reaction = gaussian(key_list[7], (S, S), S ** -0.5, 0.5)
    return {"conc": conc, "neighbours": neighbours, "counts": counts, "weights": weights, "zones": zones, "owners": owners, "rate_table": rate_table, "reaction": reaction}


def chemistry(state, reaction):
    def advance(step_index, current):
        tendency = jnp.dot(current.astype(jnp.bfloat16), reaction, preferred_element_type=jnp.float32)
        return current + 0.25 * jnp.tanh(tendency)
    return lax.fori_loop(0, SUBSTEPS, advance, state.astype(jnp.float32)).astype(jnp.bfloat16)


def reference(conc, neighbours, counts, weights, zones, owners, rate_table, reaction):
    blocks = conc.reshape(NBLOCKS, BLK, S)
    mixed = blocks
    outflow = jnp.zeros_like(blocks)
    for column in range(KADJ):
        target = neighbours[:, column]
        coef = jnp.where(column < counts, weights[:, column].astype(jnp.float32) / 128.0, 0.0)
        flux = coef[:, None, None] * (blocks[target] - blocks)
        mixed = mixed + flux
        outflow = outflow.at[target].add(flux)
    mixed = (mixed - outflow).reshape(PARCELS, S)
    photo = mixed * jnp.exp(-rate_table[zones])
    conc_out = chemistry(photo.astype(jnp.bfloat16), reaction)
    devices = N_LON * N_BAL
    owner = owners[:, 0].reshape(devices, P_DEV)
    onehot = (owner[:, :, None] == jnp.arange(N_BAL, dtype=jnp.int32)[None, None, :]).astype(jnp.int32)
    rank = jnp.sum((jnp.cumsum(onehot, axis=1) - onehot) * onehot, axis=2)
    device = jnp.arange(devices, dtype=jnp.int32)[:, None]
    band = device // N_BAL
    source = device % N_BAL
    row = (((band * N_BAL + owner) * N_BAL + source) * CAP + rank).astype(jnp.int32)
    chem_slots = jnp.zeros((SLOTS, S), jnp.bfloat16).at[row.reshape(-1)].set(conc_out)
    return conc_out, chem_slots
```

```python
import functools

import jax
import jax.numpy as jnp
from jax import lax
from jax.experimental import pallas as pl
from jax.experimental.pallas import tpu as pltpu
from jax.sharding import PartitionSpec as P

BLK = 128
LANES = 128
TILE = 16
ZONES = 32
SUBSTEPS = 12
CHUNKS = 2

F32 = jnp.float32
BF16 = jnp.bfloat16
VMEM = pl.BlockSpec(memory_space=pltpu.VMEM)
SMEM = pl.BlockSpec(memory_space=pltpu.SMEM)
ANY = pl.BlockSpec(memory_space=pl.ANY)


def iota(shape, axis):
    return lax.broadcasted_iota(jnp.int32, shape, axis)


def dot(a, b):
    return jnp.dot(a, b, preferred_element_type=F32)


def dot_first(a, b):
    return lax.dot_general(a, b, (((0,), (0,)), ((), ())), preferred_element_type=F32)


def regroup(parts, target, chunks):
    width = LANES // chunks
    group = iota(parts[0].shape, 1) // width
    out = None
    for place in range(chunks):
        moved = parts[place]
        turn = (place - target[place]) % chunks * width
        if turn:
            moved = pltpu.roll(moved, turn, 1)
        out = moved if out is None else jnp.where(group == place, moved, out)
    return out


def pack_kernel(chunks, nblocks, nbal, ndev, ids, conc, neighbours, counts, weights, *outs):
    msgs, lows, table = outs[:chunks], outs[chunks : 2 * chunks], outs[2 * chunks]
    span = BLK // chunks
    for b in range(nblocks):
        rows = [conc[b * BLK + j * span : b * BLK + (j + 1) * span, :] for j in range(chunks)]
        for c in range(chunks):
            value = regroup(rows, [c] * chunks, chunks)
            high = value.astype(BF16)
            msgs[c][b * span : (b + 1) * span, :] = high
            lows[c][b * span : (b + 1) * span, :] = (value - high.astype(F32)).astype(BF16)
    lane = iota((nblocks, LANES), 1)
    row = iota((nblocks, LANES), 0)
    pairs = jnp.zeros((nblocks, LANES), F32)
    for k in range(neighbours.shape[1]):
        target = jnp.broadcast_to(neighbours[:, k : k + 1], (nblocks, LANES))
        device = lax.div(target, nblocks)
        apart = device - ids[0]
        right = (apart == nbal) | (apart == nbal - ndev)
        column = jnp.where(apart == 0, 0, jnp.where(right, 2 * nblocks, nblocks))
        column = column + target - device * nblocks
        used = (column == lane) & (k < jnp.broadcast_to(counts[...], (nblocks, LANES)))
        weight = jnp.broadcast_to(weights[:, k : k + 1], (nblocks, LANES))
        pairs = pairs + jnp.where(used, weight, 0).astype(F32)
    pairs = jnp.where(lane == row, 0.0, pairs * (1.0 / 128.0))
    narrow = pairs.astype(BF16)

    def turned(first, place):
        eye = jnp.where(lane == row + place, 1.0, 0.0).astype(BF16)
        return dot_first(narrow, eye)[first : first + nblocks, :]

    table[...] = pairs + turned(0, 0)
    carried = turned(2 * nblocks, nblocks) + turned(nblocks, 2 * nblocks)
    msgs[0][nblocks * span : nblocks * (span + 1), :] = carried.astype(BF16)


def prepare_kernel(chunks, nblocks, nbal, ids, zones, owners, rates, *outs):
    factors, keys, bases = outs[:chunks], outs[chunks], outs[chunks + 1]
    span, width = BLK // chunks, LANES // chunks
    decay = jnp.exp(-rates[...])
    lane = iota((span, LANES), 1)
    group = lane // ZONES
    tables = []
    for c in range(chunks):
        rows = []
        for j in range(chunks):
            turn = (j - c) % chunks * width
            moved = pltpu.roll(decay, turn, 1) if turn else decay
            rows.append(jnp.where(iota(moved.shape, 1) // width == j, moved, 0.0))
        spread = jnp.concatenate(rows, axis=0)
        if chunks * ZONES < LANES:
            pad = jnp.zeros((LANES - chunks * ZONES, LANES), F32)
            spread = jnp.concatenate([spread, pad], axis=0)
        high = spread.astype(BF16)
        tables.append((high, (spread - high.astype(F32)).astype(BF16)))
    square = iota((nblocks, LANES), 0) == iota((nblocks, LANES), 1)
    upright = dot_first(zones[...].astype(F32).astype(BF16), jnp.where(square, 1.0, 0.0).astype(BF16))
    for b in range(nblocks):
        column = jnp.broadcast_to(upright[:, b : b + 1], (BLK, LANES))
        picked = column[:span]
        for j in range(1, chunks):
            picked = jnp.where(group == j, column[j * span : (j + 1) * span], picked)
        own = (picked == (lane - group * ZONES).astype(F32)) & (group < chunks)
        own = jnp.where(own, 1.0, 0.0).astype(BF16)
        for c in range(chunks):
            high, low = tables[c]
            factors[c][b] = dot(own, high) + dot(own, low)
    before = jnp.where(iota((BLK, LANES), 0) < iota((BLK, LANES), 1), 1.0, 0.0).astype(BF16)
    above = jnp.where(iota((nblocks, nblocks), 1) < iota((nblocks, nblocks), 0), 1.0, 0.0)
    table = jnp.zeros((nblocks, LANES), F32)
    slot_lane = iota((nblocks, LANES), 1)
    relative = jnp.bitwise_xor(owners[...], ids[1])
    step = TILE * chunks
    for k in range(nbal):
        mine = relative == k
        member = jnp.where(mine, 1.0, 0.0)
        narrow = member.astype(BF16)
        rank = dot(narrow, before)
        start = jnp.sum(dot(above.astype(BF16), narrow), axis=1, keepdims=True)
        window = jnp.floor(start * (1.0 / step))
        keys[k] = jnp.where(mine, rank + (start - window * step), -1.0)
        table = jnp.where(slot_lane == k, window * TILE, table)
    bases[...] = table.astype(jnp.int32)


def mix_kernel(chunks, nblocks, nbal, first, bases, *refs):
    span, width = BLK // chunks, LANES // chunks
    rows = nblocks * span
    if first:
        left, right, table, high, low, factor, keys = refs[:7]
        start, slots, full = refs[7], refs[8 : 8 + nbal], refs[8 + nbal]
        buffer = refs[9 + nbal]
    else:
        left, right, table, high, low, factor, keys = refs[:7]
        start, slots = refs[7], refs[8 : 8 + nbal]
        buffer = refs[8 + nbal]
    lane = iota((nblocks, LANES), 1)
    coupling = table[...]
    if first:
        from_left = left[rows : rows + nblocks, :].astype(F32)
        from_right = right[rows : rows + nblocks, :].astype(F32)
        coupling = coupling + jnp.where((lane >= nblocks) & (lane < 2 * nblocks), from_left, 0.0)
        coupling = coupling + jnp.where((lane >= 2 * nblocks) & (lane < 3 * nblocks), from_right, 0.0)
        full[...] = coupling
    inner = jnp.sum(jnp.where(lane < nblocks, coupling, 0.0), axis=1, keepdims=True)
    outer = jnp.sum(jnp.where(lane < nblocks, 0.0, coupling), axis=1, keepdims=True)

    def tall(value):
        value = jnp.broadcast_to(value, (nblocks, LANES))
        wide = jnp.broadcast_to(value[:, None, :], (nblocks, TILE, LANES))
        return wide.reshape(nblocks * TILE, LANES)

    keep, outer = tall(1.0 - inner), tall(outer)
    edge = nblocks * TILE
    spread = iota((LANES, 3 * edge), 1) // TILE == iota((LANES, 3 * edge), 0)
    spread = dot(tall(coupling).astype(BF16), jnp.where(spread, 1.0, 0.0).astype(BF16))
    same = iota((edge, 3 * edge), 0) % TILE == iota((edge, 3 * edge), 1) % TILE
    kron = jnp.where(same, spread, 0.0).astype(BF16)

    def part(ref, u):
        return jnp.concatenate(
            [ref[b * span + u * TILE : b * span + (u + 1) * TILE, :] for b in range(nblocks)], axis=0
        )

    for u in range(span // TILE):
        mine, rest = part(high, u), part(low, u)
        total = dot(kron[:, :edge], mine) + dot(kron[:, :edge], rest)
        total = total + dot(kron[:, edge : 2 * edge], part(left, u))
        total = total + dot(kron[:, 2 * edge :], part(right, u))
        mine = mine.astype(F32)
        total = total + keep * (mine + rest.astype(F32)) - outer * mine
        for b in range(nblocks):
            done = total[b * TILE : (b + 1) * TILE] * factor[b, u * TILE : (u + 1) * TILE, :]
            start[b, u * TILE : (u + 1) * TILE, :] = done.astype(BF16)

    reach = span + TILE
    depth = slots[0].shape[0]
    buffer[...] = jnp.zeros(buffer.shape, BF16)
    line = iota((reach, LANES), 0)
    marks = [
        (line // TILE * (TILE * chunks) + jj * TILE + line % TILE).astype(F32)
        for jj in range(chunks)
    ]
    group = iota((span, LANES), 1) // width
    for b in range(nblocks):
        select = []
        for k in range(nbal):
            key = jnp.broadcast_to(keys[k, b : b + 1, :], (reach, LANES))
            select.append(
                jnp.concatenate([jnp.where(key == m, 1.0, 0.0).astype(BF16) for m in marks], axis=1)
            )
        block = start[b].astype(F32)
        turned = [pltpu.roll(block, d * width, 1) if d else block for d in range(chunks)]
        pieces = []
        for jj in range(chunks):
            for j in range(chunks):
                piece = turned[(jj - j) % chunks]
                if chunks > 1:
                    piece = jnp.where(group == jj, piece, 0.0)
                pieces.append(piece.astype(BF16))
        placed = dot(jnp.concatenate(select, axis=0), jnp.concatenate(pieces, axis=0)).astype(BF16)
        for k in range(nbal):
            at = pl.multiple_of(bases[b, k], TILE)
            window = placed[k * reach : (k + 1) * reach]
            buffer[k, pl.ds(at, TILE), :] = buffer[k, pl.ds(at, TILE), :] + window[:TILE]
            buffer[k, pl.ds(at + TILE, span), :] = window[TILE:]
    for k in range(nbal):
        slots[k][...] = buffer[k, :depth, :]


def chemistry(state, reaction):
    def advance(_, carry):
        current = state[...]
        tendency = dot(current.astype(BF16), reaction[...])
        state[...] = current + 0.25 * jnp.tanh(tendency)
        return carry

    lax.fori_loop(0, SUBSTEPS, advance, 0)


def own_kernel(chunks, nblocks, reaction, *refs):
    starts, out, state = refs[:chunks], refs[chunks], refs[chunks + 1]
    span = BLK // chunks
    for b in range(nblocks):
        rows = [starts[c][b].astype(F32) for c in range(chunks)]
        for j in range(chunks):
            first = b * BLK + j * span
            state[first : first + span, :] = regroup(rows, [j] * chunks, chunks)
    chemistry(state, reaction)
    out[...] = state[...].astype(BF16)


def slot_kernel(chunks, nbal, ids, reaction, *refs):
    parts, out = refs[: chunks * nbal], refs[chunks * nbal]
    state, result, sem = refs[chunks * nbal + 1 :]
    depth = parts[0].shape[0]
    for k in range(nbal):
        rows = [parts[k * chunks + c][...].astype(F32) for c in range(chunks)]
        for jj in range(chunks):
            state[jj * depth : (jj + 1) * depth, :] = regroup(rows, [jj] * chunks, chunks)
        chemistry(state, reaction)
        for jj in range(chunks):
            done = state[jj * depth : (jj + 1) * depth, :].astype(BF16)
            result[k, :, jj] = done.reshape(depth // TILE, TILE, LANES)
        place = jnp.bitwise_xor(ids[1], k)
        pltpu.make_async_copy(result.at[k], out.at[place], sem.at[k]).start()
    for k in range(nbal):
        place = jnp.bitwise_xor(ids[1], k)
        pltpu.make_async_copy(result.at[k], out.at[place], sem.at[k]).wait()


def shards(conc, neighbours, counts, weights, zones, owners, rate_table, reaction):
    rows, width = conc.shape
    nblocks = rows // BLK
    nlon, nbal = lax.axis_size("lon"), lax.axis_size("bal")
    chunks = CHUNKS
    span = BLK // chunks
    capacity = 2 * rows // nbal
    depth = capacity // chunks
    bal = lax.axis_index("bal")
    ids = jnp.stack([lax.axis_index("lon") * nbal + bal, bal]).astype(jnp.int32)

    shape = jax.ShapeDtypeStruct
    packed = shape((nblocks * span, LANES), BF16)
    longer = shape((nblocks * (span + 1), LANES), BF16)
    outs = pl.pallas_call(
        functools.partial(pack_kernel, chunks, nblocks, nbal, nlon * nbal),
        out_shape=[longer] + [packed] * (2 * chunks - 1) + [shape((nblocks, LANES), F32)],
        in_specs=[SMEM] + [VMEM] * 4,
        out_specs=[VMEM] * (2 * chunks + 1),
        name="pack",
    )(ids, conc, neighbours, counts.reshape(nblocks, 1), weights)
    msgs, lows, table = outs[:chunks], outs[chunks : 2 * chunks], outs[2 * chunks]

    ahead = [(i, (i + 1) % nlon) for i in range(nlon)]
    back = [((i + 1) % nlon, i) for i in range(nlon)]
    lefts = [lax.ppermute(m, "lon", ahead) for m in msgs]
    rights = [lax.ppermute(m, "lon", back) for m in msgs]

    outs = pl.pallas_call(
        functools.partial(prepare_kernel, chunks, nblocks, nbal),
        out_shape=[shape((nblocks, span, LANES), F32)] * chunks
        + [shape((nbal, nblocks, LANES), F32), shape((nblocks, LANES), jnp.int32)],
        in_specs=[SMEM] + [VMEM] * 3,
        out_specs=[VMEM] * (chunks + 2),
        name="prepare",
    )(ids, zones.reshape(nblocks, BLK), owners.reshape(nblocks, BLK), rate_table)
    factors, keys, bases = outs[:chunks], outs[chunks], outs[chunks + 1]

    starts, received = [], [[None] * chunks for _ in range(nbal)]
    for c in range(chunks):
        first = c == 0
        outs = pl.pallas_call(
            functools.partial(mix_kernel, chunks, nblocks, nbal, first),
            out_shape=[shape((nblocks, span, LANES), BF16)]
            + [shape((depth, LANES), BF16)] * nbal
            + ([shape((nblocks, LANES), F32)] if first else []),
            in_specs=[SMEM] + [VMEM] * 7,
            out_specs=[VMEM] * (nbal + 1 + first),
            scratch_shapes=[pltpu.VMEM((nbal, depth + span + TILE, LANES), BF16)],
            name=f"mix{c}",
        )(bases, lefts[c], rights[c], table, msgs[c], lows[c], factors[c], keys)
        starts.append(outs[0])
        if first:
            table = outs[1 + nbal]
        for k in range(nbal):
            moved = outs[1 + k]
            if k:
                moved = lax.ppermute(moved, "bal", [(i, i ^ k) for i in range(nbal)])
            received[k][c] = moved

    conc_out = pl.pallas_call(
        functools.partial(own_kernel, chunks, nblocks),
        out_shape=shape((rows, LANES), BF16),
        in_specs=[VMEM] * (1 + chunks),
        out_specs=VMEM,
        scratch_shapes=[pltpu.VMEM((rows, LANES), F32)],
        name="own",
    )(reaction, *starts)

    tiles = shape((nbal, depth // TILE, chunks, TILE, LANES), BF16)
    chem_slots = pl.pallas_call(
        functools.partial(slot_kernel, chunks, nbal),
        out_shape=tiles,
        in_specs=[SMEM] + [VMEM] * (1 + chunks * nbal),
        out_specs=ANY,
        scratch_shapes=[
            pltpu.VMEM((capacity, LANES), F32),
            pltpu.VMEM(tiles.shape, BF16),
            pltpu.SemaphoreType.DMA((nbal,)),
        ],
        name="slots",
    )(ids, reaction, *[part for group in received for part in group])
    return conc_out, chem_slots.reshape(nbal * capacity, width)


def solution(mesh):
    in_specs = (
        P(("lon", "bal"), None),
        P(("lon", "bal"), None),
        P(("lon", "bal")),
        P(("lon", "bal"), None),
        P(("lon", "bal")),
        P(("lon", "bal"), None),
        P(),
        P(),
    )
    out_specs = (P(("lon", "bal"), None), P(("lon", "bal"), None))
    return jax.shard_map(shards, mesh=mesh, in_specs=in_specs, out_specs=out_specs, check_vma=False)
```

```python
import functools

import jax
import jax.numpy as jnp
from jax import lax
from jax.experimental import pallas as pl
from jax.experimental.pallas import tpu as pltpu
from jax.sharding import PartitionSpec as P


BLK = 128
LANES = 128
TILE = 16
SHIFT = 4
ZONES = 32
SUBSTEPS = 12
CHUNKS = 2
LOADS = 4
TILES = 4

F32 = jnp.float32
BF16 = jnp.bfloat16
VMEM = pl.BlockSpec(memory_space=pltpu.VMEM)
SMEM = pl.BlockSpec(memory_space=pltpu.SMEM)
ANY = pl.BlockSpec(memory_space=pl.ANY)
HBM = pl.BlockSpec(memory_space=pltpu.HBM)


def iota(shape, axis):
    return lax.broadcasted_iota(jnp.int32, shape, axis)


def dot(a, b):
    return jnp.dot(a, b, preferred_element_type=F32)


def dot_first(a, b):
    return lax.dot_general(a, b, (((0,), (0,)), ((), ())), preferred_element_type=F32)


def eye(rows, shift=0):
    shape = (rows, LANES)
    return jnp.where(iota(shape, 0) + shift == iota(shape, 1), 1.0, 0.0).astype(BF16)


def regroup(parts, source, chunks):
    width = LANES // chunks
    group = lax.shift_right_logical(iota(parts[0].shape, 1), width.bit_length() - 1)
    out = None
    for place in range(chunks):
        moved = parts[place]
        turn = (place - source) % chunks * width
        if turn:
            moved = pltpu.roll(moved, turn, 1)
        out = moved if out is None else jnp.where(group == place, moved, out)
    return out


def load_all(source, target, sems):
    rows = target.shape[0] // LOADS
    copies = [
        pltpu.make_async_copy(
            source.at[pl.ds(i * rows, rows)], target.at[pl.ds(i * rows, rows)], sems.at[i]
        )
        for i in range(LOADS)
    ]
    for copy in copies:
        copy.start()
    return copies


def pack_kernel(chunks, chunk, nblocks, conc, *refs):
    span = BLK // chunks
    if chunk == 0:
        lists, msg, table, held = refs[:3], refs[3], refs[4], refs[5:8]
        stage, buffer, sems = refs[8:]
        small = [
            pltpu.make_async_copy(source, target, sems.at[2 * LOADS + 1 + i])
            for i, (source, target) in enumerate(zip(lists, held))
        ]
        for copy in small:
            copy.start()
        neighbours, counts, weights = held
    else:
        msg, stage, buffer, sems = refs
    loads = load_all(conc, stage, sems)
    stores = []

    def store(i, first, rows):
        copy = pltpu.make_async_copy(
            buffer.at[pl.ds(first, rows)], msg.at[pl.ds(first, rows)], sems.at[LOADS + i]
        )
        copy.start()
        stores.append(copy)

    if chunk == 0:
        for copy in small:
            copy.wait()
        nlon, nbal = lax.axis_size("lon"), lax.axis_size("bal")
        me = lax.axis_index("lon") * nbal + lax.axis_index("bal")
        column = iota((3 * nblocks, nblocks), 0)
        pairs = jnp.zeros((3 * nblocks, nblocks), jnp.int32)
        for k in range(neighbours.shape[0]):
            target = neighbours[k : k + 1, :]
            device = lax.div(target, nblocks)
            apart = device - me
            right = (apart == nbal) | (apart == nbal - nlon * nbal)
            place = jnp.where(apart == 0, 0, jnp.where(right, 2 * nblocks, nblocks))
            place = place + target - device * nblocks
            weight = jnp.where(k < counts[...], weights[k : k + 1, :], 0)
            pairs = pairs + jnp.where(column == place, weight, 0)
        pairs = jnp.where(column == iota(column.shape, 1), 0, pairs)
        pairs = (pairs.astype(F32) * (1.0 / BLK)).astype(BF16)
        table[...] = dot_first(pairs, eye(3 * nblocks)) + dot(pairs[:nblocks], eye(nblocks))
        carried = dot(pairs[2 * nblocks :], eye(nblocks, nblocks))
        carried = carried + dot(pairs[nblocks : 2 * nblocks], eye(nblocks, 2 * nblocks))
        buffer[nblocks * span :, :] = carried.astype(BF16)
        store(LOADS, nblocks * span, nblocks)
    each = nblocks // LOADS
    for i in range(LOADS):
        loads[i].wait()
        for b in range(i * each, (i + 1) * each):
            rows = [stage[b * BLK + j * span : b * BLK + (j + 1) * span, :] for j in range(chunks)]
            buffer[b * span : (b + 1) * span, :] = regroup(rows, chunk, chunks).astype(BF16)
        store(i, i * each * span, each * span)
    for copy in stores:
        copy.wait()


def tall(value, rows):
    nblocks = value.shape[0]
    value = jnp.broadcast_to(value, (nblocks, LANES))
    wide = jnp.broadcast_to(value[:, None, :], (nblocks, rows, LANES))
    return wide.reshape(nblocks * rows, LANES)


def couple(table, first, blocks, nblocks):
    columns = blocks * TILE
    pick = (iota((LANES, columns), 1) >> SHIFT) + first == iota((LANES, columns), 0)
    wide = dot(table.astype(BF16), jnp.where(pick, 1.0, 0.0).astype(BF16))
    same = iota((TILE, LANES), 0) == (iota((TILE, LANES), 1) & (TILE - 1))
    same = jnp.where(same, 1.0, 0.0)
    parts = []
    for c in range(0, columns, LANES):
        part = jnp.broadcast_to(wide[:, None, c : c + LANES], (nblocks, TILE, LANES)) * same[None]
        parts.append(part.reshape(nblocks * TILE, LANES).astype(BF16))
    return jnp.concatenate(parts, axis=1)


def pieces(ref, u, nblocks, span):
    tiles = [
        jnp.concatenate(
            [ref[b * span + v * TILE : b * span + (v + 1) * TILE, :] for b in range(nblocks)], axis=0
        )
        for v in (u, u + 1)
    ]
    return jnp.concatenate(tiles, axis=1)


def prepare_kernel(chunks, chunk, nblocks, nbal, zones, rates, table, conc, *refs):
    span, width = BLK // chunks, LANES // chunks
    if chunk == 0:
        owners, factor, kept, keys, bases, stage, value, sems = refs
    else:
        factor, kept, stage, value, sems = refs
    loads = load_all(conc, stage, sems)

    decay = jnp.exp(-rates[...])
    lane = iota((span, LANES), 1)
    group = lax.shift_right_logical(lane, ZONES.bit_length() - 1)
    rows = []
    for j in range(chunks):
        turn = (j - chunk) % chunks * width
        moved = pltpu.roll(decay, turn, 1) if turn else decay
        rows.append(jnp.where(lax.shift_right_logical(iota(moved.shape, 1), width.bit_length() - 1) == j, moved, 0.0))
    if chunks * ZONES < LANES:
        rows.append(jnp.zeros((LANES - chunks * ZONES, LANES), F32))
    spread = jnp.concatenate(rows, axis=0)
    high = spread.astype(BF16)
    low = (spread - high.astype(F32)).astype(BF16)
    both = jnp.concatenate([high, low], axis=0)
    upright = dot_first(zones[...].astype(F32).astype(BF16), eye(nblocks))
    for b in range(nblocks):
        column = jnp.broadcast_to(upright[:, b : b + 1], (BLK, LANES))
        picked = column[:span]
        for j in range(1, chunks):
            picked = jnp.where(group == j, column[j * span : (j + 1) * span], picked)
        own = (picked == (lane - group * ZONES).astype(F32)) & (group < chunks)
        own = jnp.where(own, 1.0, 0.0).astype(BF16)
        factor[b] = dot(jnp.concatenate([own, own], axis=1), both)

    if chunk == 0:
        before = jnp.where(iota((BLK, LANES), 0) < iota((BLK, LANES), 1), 1.0, 0.0).astype(BF16)
        above = jnp.where(iota((nblocks, nblocks), 1) < iota((nblocks, nblocks), 0), 1.0, 0.0)
        windows = jnp.zeros((nblocks, LANES), F32)
        slot_lane = iota((nblocks, LANES), 1)
        relative = jnp.bitwise_xor(owners[...], lax.axis_index("bal"))
        step = TILE * chunks
        for k in range(nbal):
            mine = relative == k
            narrow = jnp.where(mine, 1.0, 0.0).astype(BF16)
            rank = dot(narrow, before)
            start = jnp.sum(dot(above.astype(BF16), narrow), axis=1, keepdims=True)
            window = jnp.floor(start * (1.0 / step))
            keys[k] = jnp.where(mine, rank + (start - window * step), -1.0)
            windows = jnp.where(slot_lane == k, window * TILE, windows)
        bases[...] = windows.astype(jnp.int32)

    coupling = table[...]
    kron = couple(coupling, 0, nblocks, nblocks)
    lane = iota((nblocks, LANES), 1)
    inner = jnp.sum(jnp.where(lane < nblocks, coupling, 0.0), axis=1, keepdims=True)
    keep = tall(1.0 - inner, TILE)
    each = nblocks // LOADS
    for i in range(LOADS):
        loads[i].wait()
        for b in range(i * each, (i + 1) * each):
            rows = [stage[b * BLK + j * span : b * BLK + (j + 1) * span, :] for j in range(chunks)]
            value[b * span : (b + 1) * span, :] = regroup(rows, chunk, chunks)
    for u in range(0, span // TILE, 2):
        whole = pieces(value, u, nblocks, span)
        high = whole.astype(BF16)
        low = (whole - high.astype(F32)).astype(BF16)
        total = dot(kron, high) + dot(kron, low)
        for v in range(2):
            side = slice(v * LANES, (v + 1) * LANES)
            part = total[:, side] + keep * whole[:, side]
            for b in range(nblocks):
                kept[b, (u + v) * TILE : (u + v + 1) * TILE, :] = part[b * TILE : (b + 1) * TILE]


def mix_kernel(chunks, chunk, nblocks, nbal, bases, left, right, table, high, kept, factor, keys, *refs):
    span, width = BLK // chunks, LANES // chunks
    rows = nblocks * span
    start, slots = refs[0], refs[1:nbal]
    buffer = refs[-1]
    lane = iota((nblocks, LANES), 1)
    coupling = table[...]
    if chunk == 0:
        from_left = left[rows : rows + nblocks, :].astype(F32)
        from_right = right[rows : rows + nblocks, :].astype(F32)
        coupling = coupling + jnp.where((lane >= nblocks) & (lane < 2 * nblocks), from_left, 0.0)
        coupling = coupling + jnp.where((lane >= 2 * nblocks) & (lane < 3 * nblocks), from_right, 0.0)
        refs[nbal][...] = coupling
    outer = jnp.sum(jnp.where(lane < nblocks, 0.0, coupling), axis=1, keepdims=True)
    outer = tall(outer, TILE)
    kron = couple(coupling, nblocks, 2 * nblocks, nblocks)
    edge = nblocks * TILE

    for u in range(0, span // TILE, 2):
        total = dot(kron[:, :edge], pieces(left, u, nblocks, span))
        total = total + dot(kron[:, edge:], pieces(right, u, nblocks, span))
        for v in range(2):
            at = slice((u + v) * TILE, (u + v + 1) * TILE)
            for b in range(nblocks):
                mine = high[b * span + (u + v) * TILE : b * span + (u + v + 1) * TILE, :].astype(F32)
                tile = slice(b * TILE, (b + 1) * TILE)
                mixed = total[tile, v * LANES : (v + 1) * LANES] + kept[b, at, :]
                mixed = mixed - outer[tile] * mine
                start[b, at, :] = (mixed * factor[b, at, :]).astype(BF16)

    reach = span + TILE
    depth = slots[0].shape[0]
    buffer[...] = jnp.zeros(buffer.shape, BF16)
    line = iota((reach, LANES), 0)
    marks = [
        ((line >> SHIFT) * (TILE * chunks) + jj * TILE + (line & (TILE - 1))).astype(F32)
        for jj in range(chunks)
    ]
    group = lax.shift_right_logical(iota((reach, LANES), 1), width.bit_length() - 1)
    for b in range(nblocks):
        select = []
        for k in range(1, nbal):
            key = jnp.broadcast_to(keys[k, b : b + 1, :], (reach, LANES))
            select += [jnp.where(key == m, 1.0, 0.0).astype(BF16) for m in marks]
        block = start[b].astype(F32)
        spread = [regroup([block] * chunks, j, chunks).astype(BF16) for j in range(chunks)]
        placed = dot(jnp.concatenate(select, axis=0), jnp.concatenate(spread, axis=0))
        for k in range(1, nbal):
            first = (k - 1) * chunks * reach
            window = placed[first : first + reach]
            for jj in range(1, chunks):
                other = placed[first + jj * reach : first + (jj + 1) * reach]
                window = jnp.where(group == jj, other, window)
            window = window.astype(BF16)
            at = pl.multiple_of(bases[b, k], TILE)
            buffer[k - 1, pl.ds(at, TILE), :] = buffer[k - 1, pl.ds(at, TILE), :] + window[:TILE]
            buffer[k - 1, pl.ds(at + TILE, span), :] = window[TILE:]
    for k in range(1, nbal):
        slots[k - 1][...] = buffer[k - 1, :depth, :]


def chemistry(state, reaction):
    quarter = (reaction[...].astype(F32) * 0.25).astype(BF16)
    rows = state.shape[0] // TILES
    for _ in range(SUBSTEPS):
        for t in range(TILES):
            current = state[t * rows : (t + 1) * rows, :]
            tendency = dot(current.astype(BF16), quarter)
            state[t * rows : (t + 1) * rows, :] = current + jnp.tanh(tendency)


def own_kernel(chunks, nblocks, bases, reaction, keys, *refs):
    starts, out, slots, state, done, buffer, sem = refs[:chunks], *refs[chunks:]
    span = BLK // chunks
    for b in range(nblocks):
        rows = [starts[c][b].astype(F32) * 4.0 for c in range(chunks)]
        for j in range(chunks):
            first = b * BLK + j * span
            state[first : first + span, :] = regroup(rows, j, chunks)
    chemistry(state, reaction)
    done[...] = (state[...] * 0.25).astype(BF16)
    out[...] = done[...]
    reach = BLK + TILE * chunks
    capacity = slots.shape[1] * slots.shape[2] * slots.shape[3]
    buffer[...] = jnp.zeros(buffer.shape, BF16)
    mark = iota((reach, LANES), 0).astype(F32)
    for b in range(nblocks):
        key = jnp.broadcast_to(keys[0, b : b + 1, :], (reach, LANES))
        select = jnp.where(key == mark, 1.0, 0.0).astype(BF16)
        window = dot(select, done[b * BLK : (b + 1) * BLK, :]).astype(BF16)
        at = pl.multiple_of(bases[b, 0] * chunks, TILE)
        edge = TILE * chunks
        buffer[pl.ds(at, edge), :] = buffer[pl.ds(at, edge), :] + window[:edge]
        buffer[pl.ds(at + edge, BLK), :] = window[edge:]
    for _ in range(1):
        copy = pltpu.make_async_copy(
            buffer.at[pl.ds(0, capacity)].reshape(slots.shape[1:]), slots.at[lax.axis_index("bal")], sem
        )
        copy.start()
        copy.wait()


def slot_kernel(chunks, k, reaction, *refs):
    parts = refs[:chunks]
    out, state, result, sem = refs[-4:]
    depth = parts[0].shape[0]
    rows = [part[...].astype(F32) * 4.0 for part in parts]
    for jj in range(chunks):
        state[jj * depth : (jj + 1) * depth, :] = regroup(rows, jj, chunks)
    chemistry(state, reaction)
    for jj in range(chunks):
        done = (state[jj * depth : (jj + 1) * depth, :] * 0.25).astype(BF16)
        result[:, jj] = done.reshape(depth // TILE, TILE, LANES)
    place = jnp.bitwise_xor(lax.axis_index("bal"), k)
    copy = pltpu.make_async_copy(result, out.at[place], sem)
    copy.start()
    copy.wait()


def ORDER(nbal):
    return [k for k in range(1, nbal) if k != 2] + [2]


def step(conc, neighbours, counts, weights, zones, owners, rate_table, reaction):
    rows, width = conc.shape
    nblocks = rows // BLK
    nlon, nbal = lax.axis_size("lon"), lax.axis_size("bal")
    chunks = CHUNKS
    span = BLK // chunks
    capacity = 2 * rows // nbal
    depth = capacity // chunks

    shape = jax.ShapeDtypeStruct
    zones, owners = zones.reshape(nblocks, BLK), owners.reshape(nblocks, BLK)
    blocked = shape((nblocks, span, LANES), F32)

    def call(body, limit=16, **kw):
        params = pltpu.CompilerParams(vmem_limit_bytes=limit << 20)
        return pl.pallas_call(body, compiler_params=params, **kw)

    ahead = [(i, (i + 1) % nlon) for i in range(nlon)]
    back = [((i + 1) % nlon, i) for i in range(nlon)]
    lists = (neighbours.T, counts.reshape(1, nblocks), weights.T)
    msgs, lefts, rights, table = [], [], [], None
    for c in range(chunks):
        first = c == 0
        length = nblocks * span + (nblocks if first else 0)
        outs = call(
            functools.partial(pack_kernel, chunks, c, nblocks),
            60 if first else 16,
            out_shape=[shape((length, LANES), BF16)] + [shape((nblocks, LANES), F32)] * first,
            in_specs=[HBM] * (1 + 3 * first),
            out_specs=[ANY] + [VMEM] * first,
            scratch_shapes=[pltpu.VMEM(a.shape, jnp.int32) for a in lists if first]
            + [
                pltpu.VMEM((rows, LANES), F32),
                pltpu.VMEM((length, LANES), BF16),
                pltpu.SemaphoreType.DMA((2 * LOADS + 4,)),
            ],
        )(conc, *(lists if first else ()))
        if first:
            table = outs[1]
        msgs.append(outs[0])
        lefts.append(lax.ppermute(outs[0], "lon", ahead))
        rights.append(lax.ppermute(outs[0], "lon", back))

    factors, kepts, keys, bases = [], [], None, None
    for c in range(chunks):
        first = c == 0
        outs = call(
            functools.partial(prepare_kernel, chunks, c, nblocks, nbal),
            out_shape=[blocked, blocked]
            + [shape((nbal, nblocks, LANES), F32), shape((nblocks, LANES), jnp.int32)] * first,
            in_specs=[VMEM] * 3 + [HBM] + [VMEM] * first,
            out_specs=[VMEM] * (2 + 2 * first),
            scratch_shapes=[
                pltpu.VMEM((rows, LANES), F32),
                pltpu.VMEM((nblocks * span, LANES), F32),
                pltpu.SemaphoreType.DMA((LOADS,)),
            ],
        )(zones, rate_table, table, conc, *([owners] if first else []))
        factors.append(outs[0])
        kepts.append(outs[1])
        if first:
            keys, bases = outs[2:]

    starts, received = [], [[None] * chunks for _ in range(nbal)]
    for c in range(chunks):
        first = c == 0
        outs = call(
            functools.partial(mix_kernel, chunks, c, nblocks, nbal),
            out_shape=[shape((nblocks, span, LANES), BF16)]
            + [shape((depth, LANES), BF16)] * (nbal - 1)
            + [shape((nblocks, LANES), F32)] * first,
            in_specs=[SMEM] + [VMEM] * 7,
            out_specs=[VMEM] * (nbal + first),
            scratch_shapes=[pltpu.VMEM((nbal - 1, depth + span + TILE, LANES), BF16)],
        )(bases, lefts[c], rights[c], table, msgs[c], kepts[c], factors[c], keys)
        starts.append(outs[0])
        if first:
            table = outs[nbal]
        for k in range(1, nbal):
            received[k][c] = lax.ppermute(outs[k], "bal", [(i, i ^ k) for i in range(nbal)])

    tiles = shape((nbal, depth // TILE, chunks, TILE, LANES), BF16)
    conc_out, chem = call(
        functools.partial(own_kernel, chunks, nblocks),
        out_shape=[shape((rows, LANES), BF16), tiles],
        in_specs=[SMEM] + [VMEM] * (2 + chunks),
        out_specs=[VMEM, ANY],
        scratch_shapes=[
            pltpu.VMEM((rows, LANES), F32),
            pltpu.VMEM((rows, LANES), BF16),
            pltpu.VMEM((capacity + BLK + TILE * chunks, LANES), BF16),
            pltpu.SemaphoreType.DMA,
        ],
    )(bases, reaction, keys, *starts)
    for k in ORDER(nbal):
        chem = call(
            functools.partial(slot_kernel, chunks, k),
            out_shape=tiles,
            in_specs=[VMEM] * (1 + chunks) + [ANY],
            out_specs=ANY,
            scratch_shapes=[
                pltpu.VMEM((capacity, LANES), F32),
                pltpu.VMEM(tiles.shape[1:], BF16),
                pltpu.SemaphoreType.DMA,
            ],
            input_output_aliases={1 + chunks: 0},
        )(reaction, *received[k], chem)
    return conc_out, chem.reshape(nbal * capacity, width)


def solution(mesh):
    in_specs = (
        P(("lon", "bal"), None),
        P(("lon", "bal"), None),
        P(("lon", "bal")),
        P(("lon", "bal"), None),
        P(("lon", "bal")),
        P(("lon", "bal"), None),
        P(),
        P(),
    )
    out_specs = (P(("lon", "bal"), None), P(("lon", "bal"), None))
    return jax.shard_map(step, mesh=mesh, in_specs=in_specs, out_specs=out_specs, check_vma=False)
```

```python
import functools

import jax
import jax.numpy as jnp
from jax import lax
from jax.experimental import pallas as pl
from jax.experimental.pallas import tpu as pltpu
from jax.sharding import PartitionSpec as P


BLK = 128
LANES = 128
TILE = 16
SHIFT = 4
ZONES = 32
SUBSTEPS = 12
CHUNKS = 2
LOADS = 4
TILES = 4
LATE = 4

F32 = jnp.float32
BF16 = jnp.bfloat16
VMEM = pl.BlockSpec(memory_space=pltpu.VMEM)
ANY = pl.BlockSpec(memory_space=pl.ANY)
HBM = pl.BlockSpec(memory_space=pltpu.HBM)


def iota(shape, axis):
    return lax.broadcasted_iota(jnp.int32, shape, axis)


def dot(a, b):
    return jnp.dot(a, b, preferred_element_type=F32)


def dot_first(a, b):
    return lax.dot_general(a, b, (((0,), (0,)), ((), ())), preferred_element_type=F32)


def eye(rows, shift=0):
    shape = (rows, LANES)
    return jnp.where(iota(shape, 0) + shift == iota(shape, 1), 1.0, 0.0).astype(BF16)


def regroup(parts, source, chunks):
    width = LANES // chunks
    group = lax.shift_right_logical(iota(parts[0].shape, 1), width.bit_length() - 1)
    out = None
    for place in range(chunks):
        moved = parts[place]
        turn = (place - source) % chunks * width
        if turn:
            moved = pltpu.roll(moved, turn, 1)
        out = moved if out is None else jnp.where(group == place, moved, out)
    return out


def load_all(source, target, sems):
    rows = target.shape[0] // LOADS
    copies = [
        pltpu.make_async_copy(
            source.at[pl.ds(i * rows, rows)], target.at[pl.ds(i * rows, rows)], sems.at[i]
        )
        for i in range(LOADS)
    ]
    for copy in copies:
        copy.start()
    return copies


def pack_kernel(chunks, chunk, nblocks, conc, *refs):
    span = BLK // chunks
    loads, stage = [], conc
    if chunk == 0:
        lists, msg, table, stage, held, sems = refs[:3], *refs[3:6], refs[6:9], refs[9]
        small = [
            pltpu.make_async_copy(source, target, sems.at[LOADS + i])
            for i, (source, target) in enumerate(zip(lists, held))
        ]
        for copy in small:
            copy.start()
        loads = load_all(conc, stage, sems)
        for copy in small:
            copy.wait()
        neighbours, counts, weights = held
        nlon, nbal = lax.axis_size("lon"), lax.axis_size("bal")
        me = lax.axis_index("lon") * nbal + lax.axis_index("bal")
        column = iota((3 * nblocks, nblocks), 0)
        pairs = jnp.zeros((3 * nblocks, nblocks), jnp.int32)
        for k in range(neighbours.shape[0]):
            target = neighbours[k : k + 1, :]
            device = lax.div(target, nblocks)
            apart = device - me
            right = (apart == nbal) | (apart == nbal - nlon * nbal)
            place = jnp.where(apart == 0, 0, jnp.where(right, 2 * nblocks, nblocks))
            place = place + target - device * nblocks
            weight = jnp.where(k < counts[...], weights[k : k + 1, :], 0)
            pairs = pairs + jnp.where(column == place, weight, 0)
        pairs = jnp.where(column == iota(column.shape, 1), 0, pairs)
        pairs = (pairs.astype(F32) * (1.0 / BLK)).astype(BF16)
        table[...] = dot_first(pairs, eye(3 * nblocks)) + dot(pairs[:nblocks], eye(nblocks))
        carried = dot(pairs[2 * nblocks :], eye(nblocks, nblocks))
        carried = carried + dot(pairs[nblocks : 2 * nblocks], eye(nblocks, 2 * nblocks))
        msg[nblocks * span :, :] = carried.astype(BF16)
    else:
        (msg,) = refs
    each = nblocks // LOADS
    for b in range(nblocks):
        if loads and b % each == 0:
            loads[b // each].wait()
        rows = [stage[b * BLK + j * span : b * BLK + (j + 1) * span, :] for j in range(chunks)]
        rows = [row.astype(BF16) for row in rows]
        msg[b * span : (b + 1) * span, :] = regroup(rows, chunk, chunks)


def tall(value, rows):
    nblocks = value.shape[0]
    value = jnp.broadcast_to(value, (nblocks, LANES))
    wide = jnp.broadcast_to(value[:, None, :], (nblocks, rows, LANES))
    return wide.reshape(nblocks * rows, LANES)


def couple(table, first, blocks, nblocks):
    columns = blocks * TILE
    pick = (iota((LANES, columns), 1) >> SHIFT) + first == iota((LANES, columns), 0)
    wide = dot(table.astype(BF16), jnp.where(pick, 1.0, 0.0).astype(BF16))
    same = iota((TILE, LANES), 0) == (iota((TILE, LANES), 1) & (TILE - 1))
    same = jnp.where(same, 1.0, 0.0)
    parts = []
    for c in range(0, columns, LANES):
        part = jnp.broadcast_to(wide[:, None, c : c + LANES], (nblocks, TILE, LANES)) * same[None]
        parts.append(part.reshape(nblocks * TILE, LANES).astype(BF16))
    return jnp.concatenate(parts, axis=1)


def pieces(ref, u, nblocks, span):
    tiles = [
        jnp.concatenate(
            [ref[b * span + v * TILE : b * span + (v + 1) * TILE, :] for b in range(nblocks)], axis=0
        )
        for v in (u, u + 1)
    ]
    return jnp.concatenate(tiles, axis=1)


def prepare_kernel(chunks, chunk, nblocks, nbal, zones, rates, table, conc, *refs):
    span, width = BLK // chunks, LANES // chunks
    if chunk == 0:
        owners, factor, kept, keys, bases, value = refs
    else:
        factor, kept, value = refs

    decay = jnp.exp(-rates[...])
    lane = iota((span, LANES), 1)
    group = lax.shift_right_logical(lane, ZONES.bit_length() - 1)
    rows = []
    for j in range(chunks):
        turn = (j - chunk) % chunks * width
        moved = pltpu.roll(decay, turn, 1) if turn else decay
        rows.append(jnp.where(lax.shift_right_logical(iota(moved.shape, 1), width.bit_length() - 1) == j, moved, 0.0))
    if chunks * ZONES < LANES:
        rows.append(jnp.zeros((LANES - chunks * ZONES, LANES), F32))
    spread = jnp.concatenate(rows, axis=0)
    high = spread.astype(BF16)
    low = (spread - high.astype(F32)).astype(BF16)
    both = jnp.concatenate([high, low], axis=0)
    upright = dot_first(zones[...].astype(F32).astype(BF16), eye(nblocks))
    for b in range(nblocks):
        column = jnp.broadcast_to(upright[:, b : b + 1], (BLK, LANES))
        picked = column[:span]
        for j in range(1, chunks):
            picked = jnp.where(group == j, column[j * span : (j + 1) * span], picked)
        own = (picked == (lane - group * ZONES).astype(F32)) & (group < chunks)
        own = jnp.where(own, 1.0, 0.0).astype(BF16)
        factor[b] = dot(jnp.concatenate([own, own], axis=1), both)

    if chunk == 0:
        before = jnp.where(iota((BLK, LANES), 0) < iota((BLK, LANES), 1), 1.0, 0.0).astype(BF16)
        above = jnp.where(iota((nblocks, nblocks), 1) < iota((nblocks, nblocks), 0), 1.0, 0.0)
        windows = jnp.zeros((nblocks, LANES), F32)
        slot_lane = iota((nblocks, LANES), 1)
        relative = jnp.bitwise_xor(owners[...], lax.axis_index("bal"))
        step = TILE * chunks
        for k in range(nbal):
            mine = relative == k
            narrow = jnp.where(mine, 1.0, 0.0).astype(BF16)
            rank = dot(narrow, before)
            start = jnp.sum(dot(above.astype(BF16), narrow), axis=1, keepdims=True)
            window = jnp.floor(start * (1.0 / step))
            keys[k] = jnp.where(mine, rank + (start - window * step), -1.0)
            windows = jnp.where(slot_lane == k, window * TILE, windows)
        bases[...] = windows.astype(jnp.int32)

    coupling = table[...]
    kron = couple(coupling, 0, nblocks, nblocks)
    lane = iota((nblocks, LANES), 1)
    inner = jnp.sum(jnp.where(lane < nblocks, coupling, 0.0), axis=1, keepdims=True)
    keep = tall(1.0 - inner, TILE)
    for b in range(nblocks):
        rows = [conc[b * BLK + j * span : b * BLK + (j + 1) * span, :] for j in range(chunks)]
        value[b * span : (b + 1) * span, :] = regroup(rows, chunk, chunks)
    for u in range(0, span // TILE, 2):
        whole = pieces(value, u, nblocks, span)
        high = whole.astype(BF16)
        low = (whole - high.astype(F32)).astype(BF16)
        total = dot(kron, high) + dot(kron, low)
        for v in range(2):
            side = slice(v * LANES, (v + 1) * LANES)
            part = total[:, side] + keep * whole[:, side]
            for b in range(nblocks):
                kept[b, (u + v) * TILE : (u + v + 1) * TILE, :] = part[b * TILE : (b + 1) * TILE]


def mix_kernel(chunks, chunk, nblocks, nbal, bases, left, right, table, high, kept, factor, keys, *refs):
    span, width = BLK // chunks, LANES // chunks
    rows = nblocks * span
    start, slots = refs[0], refs[1:nbal]
    buffer, places, sem = refs[-3:]
    copy = pltpu.make_async_copy(bases, places, sem)
    copy.start()
    lane = iota((nblocks, LANES), 1)
    coupling = table[...]
    if chunk == 0:
        from_left = left[rows : rows + nblocks, :].astype(F32)
        from_right = right[rows : rows + nblocks, :].astype(F32)
        coupling = coupling + jnp.where((lane >= nblocks) & (lane < 2 * nblocks), from_left, 0.0)
        coupling = coupling + jnp.where((lane >= 2 * nblocks) & (lane < 3 * nblocks), from_right, 0.0)
        refs[nbal][...] = coupling
    outer = jnp.sum(jnp.where(lane < nblocks, 0.0, coupling), axis=1, keepdims=True)
    outer = tall(outer, TILE)
    kron = couple(coupling, nblocks, 2 * nblocks, nblocks)
    edge = nblocks * TILE

    for u in range(0, span // TILE, 2):
        total = dot(kron[:, :edge], pieces(left, u, nblocks, span))
        total = total + dot(kron[:, edge:], pieces(right, u, nblocks, span))
        for v in range(2):
            at = slice((u + v) * TILE, (u + v + 1) * TILE)
            for b in range(nblocks):
                mine = high[b * span + (u + v) * TILE : b * span + (u + v + 1) * TILE, :].astype(F32)
                tile = slice(b * TILE, (b + 1) * TILE)
                mixed = total[tile, v * LANES : (v + 1) * LANES] + kept[b, at, :]
                mixed = mixed - outer[tile] * mine
                start[b, at, :] = (mixed * factor[b, at, :]).astype(BF16)

    reach = span + TILE
    depth = slots[0].shape[0]
    buffer[...] = jnp.zeros(buffer.shape, BF16)
    line = iota((reach, LANES), 0)
    marks = [
        ((line >> SHIFT) * (TILE * chunks) + jj * TILE + (line & (TILE - 1))).astype(F32)
        for jj in range(chunks)
    ]
    group = lax.shift_right_logical(iota((reach, LANES), 1), width.bit_length() - 1)
    copy.wait()
    for b in range(nblocks):
        select = []
        for k in range(1, nbal):
            key = jnp.broadcast_to(keys[k, b : b + 1, :], (reach, LANES))
            select += [jnp.where(key == m, 1.0, 0.0).astype(BF16) for m in marks]
        spread = [regroup([start[b]] * chunks, j, chunks) for j in range(chunks)]
        placed = dot(jnp.concatenate(select, axis=0), jnp.concatenate(spread, axis=0))
        for k in range(1, nbal):
            first = (k - 1) * chunks * reach
            window = placed[first : first + reach]
            for jj in range(1, chunks):
                other = placed[first + jj * reach : first + (jj + 1) * reach]
                window = jnp.where(group == jj, other, window)
            window = window.astype(BF16)
            at = pl.multiple_of(jnp.minimum(places[b, k], depth), TILE)
            buffer[k - 1, pl.ds(at, TILE), :] = buffer[k - 1, pl.ds(at, TILE), :] + window[:TILE]
            buffer[k - 1, pl.ds(at + TILE, span), :] = window[TILE:]
    for k in range(1, nbal):
        slots[k - 1][...] = buffer[k - 1, :depth, :]


def chemistry(state, reaction):
    quarter = (reaction[...].astype(F32) * 0.25).astype(BF16)
    rows = state.shape[0] // TILES
    for _ in range(SUBSTEPS):
        for t in range(TILES):
            current = state[t * rows : (t + 1) * rows, :]
            tendency = dot(current.astype(BF16), quarter)
            state[t * rows : (t + 1) * rows, :] = current + jnp.tanh(tendency)


def own_kernel(chunks, nblocks, nbal, bases, reaction, keys, *refs):
    starts, out, slots, lates = refs[:chunks], refs[chunks], refs[chunks + 1], refs[chunks + 2 : -6]
    state, done, mine, others, places, sems = refs[-6:]
    copy = pltpu.make_async_copy(bases, places, sems.at[2])
    copy.start()
    span, capacity, late = BLK // chunks, slots.shape[1], lates[0].shape[0]
    for b in range(nblocks):
        for j in range(chunks):
            first = b * BLK + j * span
            rows = regroup([starts[c][b] for c in range(chunks)], j, chunks)
            state[first : first + span, :] = rows.astype(F32) * 4.0
    chemistry(state, reaction)
    done[...] = (state[...] * 0.25).astype(BF16)
    result = pltpu.make_async_copy(done, out, sems.at[0])
    result.start()
    edge = TILE * chunks
    reach = BLK + edge
    mine[...] = jnp.zeros(mine.shape, BF16)
    others[...] = jnp.zeros(others.shape, BF16)
    mark = iota((reach, LANES), 0).astype(F32)
    copy.wait()
    for b in range(nblocks):
        select = []
        for k in range(nbal):
            key = jnp.broadcast_to(keys[k, b : b + 1, :], (reach, LANES))
            select.append(jnp.where(key == mark, 1.0, 0.0).astype(BF16))
        placed = dot(jnp.concatenate(select, axis=0), done[b * BLK : (b + 1) * BLK, :]).astype(BF16)
        for k in range(nbal):
            at = places[b, k] * chunks
            target = mine
            if k:
                at = jnp.maximum(at - (capacity - late - reach), 0)
                target = others.at[k - 1]
            at = pl.multiple_of(at, TILE)
            window = placed[k * reach : (k + 1) * reach]
            target[pl.ds(at, edge), :] = target[pl.ds(at, edge), :] + window[:edge]
            target[pl.ds(at + edge, BLK), :] = window[edge:]
    own = pltpu.make_async_copy(
        mine.at[pl.ds(0, capacity)], slots.at[lax.axis_index("bal")], sems.at[1]
    )
    own.start()
    for k in range(1, nbal):
        lates[k - 1][...] = others[k - 1, reach : reach + late, :]
    result.wait()
    own.wait()


def slot_kernel(chunks, nbal, reaction, *refs):
    parts = refs[: (nbal - 1) * chunks]
    out, state, result, sems = refs[-4:]
    depth = parts[0].shape[0]
    early = depth * chunks
    for k in range(1, nbal):
        mine = parts[(k - 1) * chunks : k * chunks]
        for jj in range(chunks):
            first = (k - 1) * early + jj * depth
            rows = regroup([part[...] for part in mine], jj, chunks)
            state[first : first + depth, :] = rows.astype(F32) * 4.0
    chemistry(state, reaction)
    copies = []
    for k in range(1, nbal):
        for jj in range(chunks):
            first = (k - 1) * early + jj * depth
            done = (state[first : first + depth, :] * 0.25).astype(BF16)
            result[k - 1, :, jj] = done.reshape(depth // TILE, TILE, LANES)
        place = jnp.bitwise_xor(lax.axis_index("bal"), k)
        copies.append(
            pltpu.make_async_copy(
                result.at[k - 1].reshape(early, LANES),
                out.at[place, pl.ds(0, early)],
                sems.at[k - 1],
            )
        )
        copies[-1].start()
    for copy in copies:
        copy.wait()


def late_kernel(nbal, *refs):
    lates, out, sems = refs[: nbal - 1], refs[-2], refs[-1]
    late = lates[0].shape[0]
    copies = []
    for k in range(1, nbal):
        place = jnp.bitwise_xor(lax.axis_index("bal"), k)
        target = out.at[place, pl.ds(out.shape[1] - late, late)]
        copies.append(pltpu.make_async_copy(lates[k - 1], target, sems.at[k - 1]))
        copies[-1].start()
    for copy in copies:
        copy.wait()


def step(conc, neighbours, counts, weights, zones, owners, rate_table, reaction):
    rows, width = conc.shape
    nblocks = rows // BLK
    nlon, nbal = lax.axis_size("lon"), lax.axis_size("bal")
    chunks = CHUNKS
    span = BLK // chunks
    capacity = 2 * rows // nbal
    late = capacity // LATE
    depth = (capacity - late) // chunks

    shape = jax.ShapeDtypeStruct
    zones, owners = zones.reshape(nblocks, BLK), owners.reshape(nblocks, BLK)
    blocked = shape((nblocks, span, LANES), F32)

    def call(body, **kw):
        params = pltpu.CompilerParams(vmem_limit_bytes=16 << 20)
        return pl.pallas_call(body, compiler_params=params, **kw)

    def in_hbm(array):
        return pltpu.with_memory_space_constraint(array, pltpu.HBM)

    ahead = [(i, (i + 1) % nlon) for i in range(nlon)]
    back = [((i + 1) % nlon, i) for i in range(nlon)]
    lists = (neighbours.T, counts.reshape(1, nblocks), weights.T)
    msgs, lefts, rights, table = [], [], [], None
    for c in range(chunks):
        first = c == 0
        length = nblocks * span + (nblocks if first else 0)
        outs = call(
            functools.partial(pack_kernel, chunks, c, nblocks),
            out_shape=[shape((length, LANES), BF16)]
            + [shape((nblocks, LANES), F32), shape((rows, LANES), F32)] * first,
            in_specs=[HBM] * 4 if first else [VMEM],
            out_specs=[VMEM] * (1 + 2 * first),
            scratch_shapes=[pltpu.VMEM(a.shape, jnp.int32) for a in lists if first]
            + [pltpu.SemaphoreType.DMA((LOADS + 3,))] * first,
        )(*((in_hbm(conc), *map(in_hbm, lists)) if first else (stage,)))
        if first:
            table, stage = outs[1:]
        msgs.append(outs[0])
        lefts.append(lax.ppermute(outs[0], "lon", ahead))
        rights.append(lax.ppermute(outs[0], "lon", back))

    factors, kepts, keys, bases = [], [], None, None
    for c in range(chunks):
        first = c == 0
        outs = call(
            functools.partial(prepare_kernel, chunks, c, nblocks, nbal),
            out_shape=[blocked, blocked]
            + [shape((nbal, nblocks, LANES), F32), shape((nblocks, LANES), jnp.int32)] * first,
            in_specs=[VMEM] * (4 + first),
            out_specs=[VMEM] * (2 + 2 * first),
            scratch_shapes=[pltpu.VMEM((nblocks * span, LANES), F32)],
        )(zones, rate_table, table, stage, *([owners] if first else []))
        factors.append(outs[0])
        kepts.append(outs[1])
        if first:
            keys, bases = outs[2:]

    starts, received = [], [[None] * chunks for _ in range(nbal)]
    for c in range(chunks):
        first = c == 0
        outs = call(
            functools.partial(mix_kernel, chunks, c, nblocks, nbal),
            out_shape=[shape((nblocks, span, LANES), BF16)]
            + [shape((depth, LANES), BF16)] * (nbal - 1)
            + [shape((nblocks, LANES), F32)] * first,
            in_specs=[VMEM] * 8,
            out_specs=[VMEM] * (nbal + first),
            scratch_shapes=[
                pltpu.VMEM((nbal - 1, depth + span + TILE, LANES), BF16),
                pltpu.SMEM(bases.shape, jnp.int32),
                pltpu.SemaphoreType.DMA,
            ],
        )(bases, lefts[c], rights[c], table, msgs[c], kepts[c], factors[c], keys)
        starts.append(outs[0])
        if first:
            table = outs[nbal]
        for k in range(1, nbal):
            received[k][c] = lax.ppermute(outs[k], "bal", [(i, i ^ k) for i in range(nbal)])

    slots = shape((nbal, capacity, LANES), BF16)
    reach = BLK + TILE * chunks
    conc_out, chem, *lates = call(
        functools.partial(own_kernel, chunks, nblocks, nbal),
        out_shape=[shape((rows, LANES), BF16), slots] + [shape((late, LANES), BF16)] * (nbal - 1),
        in_specs=[VMEM] * (3 + chunks),
        out_specs=[ANY, ANY] + [VMEM] * (nbal - 1),
        scratch_shapes=[
            pltpu.VMEM((rows, LANES), F32),
            pltpu.VMEM((rows, LANES), BF16),
            pltpu.VMEM((capacity + reach, LANES), BF16),
            pltpu.VMEM((nbal - 1, late + 2 * reach, LANES), BF16),
            pltpu.SMEM(bases.shape, jnp.int32),
            pltpu.SemaphoreType.DMA((3,)),
        ],
    )(bases, reaction, keys, *starts)
    for k in range(1, nbal):
        moved = lax.ppermute(lates[k - 1], "bal", [(i, i ^ k) for i in range(nbal)])
        lates[k - 1] = moved
    chem = call(
        functools.partial(slot_kernel, chunks, nbal),
        out_shape=slots,
        in_specs=[VMEM] * (1 + chunks * (nbal - 1)) + [ANY],
        out_specs=ANY,
        scratch_shapes=[
            pltpu.VMEM(((nbal - 1) * (capacity - late), LANES), F32),
            pltpu.VMEM((nbal - 1, depth // TILE, chunks, TILE, LANES), BF16),
            pltpu.SemaphoreType.DMA((nbal - 1,)),
        ],
        input_output_aliases={1 + chunks * (nbal - 1): 0},
    )(reaction, *[part for group in received[1:] for part in group], chem)
    chem = call(
        functools.partial(late_kernel, nbal),
        out_shape=slots,
        in_specs=[VMEM] * (nbal - 1) + [ANY],
        out_specs=ANY,
        scratch_shapes=[pltpu.SemaphoreType.DMA((nbal - 1,))],
        input_output_aliases={nbal - 1: 0},
    )(*lates, chem)
    return conc_out, chem.reshape(nbal * capacity, width)


def solution(mesh):
    in_specs = (
        P(("lon", "bal"), None),
        P(("lon", "bal"), None),
        P(("lon", "bal")),
        P(("lon", "bal"), None),
        P(("lon", "bal")),
        P(("lon", "bal"), None),
        P(),
        P(),
    )
    out_specs = (P(("lon", "bal"), None), P(("lon", "bal"), None))
    return jax.shard_map(step, mesh=mesh, in_specs=in_specs, out_specs=out_specs, check_vma=False)
```

```python
import functools

import jax
import jax.numpy as jnp
from jax import lax
from jax.experimental import pallas as pl
from jax.experimental.pallas import tpu as pltpu
from jax.sharding import PartitionSpec as P


BLK = 128
LANES = 128
TILE = 16
SHIFT = 4
ZONES = 32
SUBSTEPS = 12
CHUNKS = 2
LOADS = 4
TILES = 4
LATE = 6

F32 = jnp.float32
BF16 = jnp.bfloat16
VMEM = pl.BlockSpec(memory_space=pltpu.VMEM)
ANY = pl.BlockSpec(memory_space=pl.ANY)
HBM = pl.BlockSpec(memory_space=pltpu.HBM)


def iota(shape, axis):
    return lax.broadcasted_iota(jnp.int32, shape, axis)


def dot(a, b):
    return jnp.dot(a, b, preferred_element_type=F32)


def dot_first(a, b):
    return lax.dot_general(a, b, (((0,), (0,)), ((), ())), preferred_element_type=F32)


def eye(rows, shift=0):
    shape = (rows, LANES)
    return jnp.where(iota(shape, 0) + shift == iota(shape, 1), 1.0, 0.0).astype(BF16)


def regroup(parts, source, chunks):
    width = LANES // chunks
    group = lax.shift_right_logical(iota(parts[0].shape, 1), width.bit_length() - 1)
    out = None
    for place in range(chunks):
        moved = parts[place]
        turn = (place - source) % chunks * width
        if turn:
            moved = pltpu.roll(moved, turn, 1)
        out = moved if out is None else jnp.where(group == place, moved, out)
    return out


def load_all(source, target, sems):
    rows = target.shape[0] // LOADS
    copies = [
        pltpu.make_async_copy(
            source.at[pl.ds(i * rows, rows)], target.at[pl.ds(i * rows, rows)], sems.at[i]
        )
        for i in range(LOADS)
    ]
    for copy in copies:
        copy.start()
    return copies


def pack_kernel(chunks, chunk, nblocks, conc, *refs):
    span = BLK // chunks
    loads, stage = [], conc
    if chunk == 0:
        lists, msg, table, stage, held, sems = refs[:3], *refs[3:6], refs[6:9], refs[9]
        small = [
            pltpu.make_async_copy(source, target, sems.at[LOADS + i])
            for i, (source, target) in enumerate(zip(lists, held))
        ]
        for copy in small:
            copy.start()
        loads = load_all(conc, stage, sems)
        for copy in small:
            copy.wait()
        neighbours, counts, weights = held
        nlon, nbal = lax.axis_size("lon"), lax.axis_size("bal")
        me = lax.axis_index("lon") * nbal + lax.axis_index("bal")
        column = iota((3 * nblocks, nblocks), 0)
        pairs = jnp.zeros((3 * nblocks, nblocks), jnp.int32)
        for k in range(neighbours.shape[0]):
            target = neighbours[k : k + 1, :]
            device = lax.div(target, nblocks)
            apart = device - me
            right = (apart == nbal) | (apart == nbal - nlon * nbal)
            place = jnp.where(apart == 0, 0, jnp.where(right, 2 * nblocks, nblocks))
            place = place + target - device * nblocks
            weight = jnp.where(k < counts[...], weights[k : k + 1, :], 0)
            pairs = pairs + jnp.where(column == place, weight, 0)
        pairs = jnp.where(column == iota(column.shape, 1), 0, pairs)
        pairs = (pairs.astype(F32) * (1.0 / BLK)).astype(BF16)
        table[...] = dot_first(pairs, eye(3 * nblocks)) + dot(pairs[:nblocks], eye(nblocks))
        carried = dot(pairs[2 * nblocks :], eye(nblocks, nblocks))
        carried = carried + dot(pairs[nblocks : 2 * nblocks], eye(nblocks, 2 * nblocks))
        msg[nblocks * span :, :] = carried.astype(BF16)
    else:
        (msg,) = refs
    each = nblocks // LOADS
    for b in range(nblocks):
        if loads and b % each == 0:
            loads[b // each].wait()
        rows = [stage[b * BLK + j * span : b * BLK + (j + 1) * span, :] for j in range(chunks)]
        rows = [row.astype(BF16) for row in rows]
        msg[b * span : (b + 1) * span, :] = regroup(rows, chunk, chunks)


def tall(value, rows):
    nblocks = value.shape[0]
    value = jnp.broadcast_to(value, (nblocks, LANES))
    wide = jnp.broadcast_to(value[:, None, :], (nblocks, rows, LANES))
    return wide.reshape(nblocks * rows, LANES)


def couple(table, first, blocks, nblocks):
    columns = blocks * TILE
    pick = (iota((LANES, columns), 1) >> SHIFT) + first == iota((LANES, columns), 0)
    wide = dot(table.astype(BF16), jnp.where(pick, 1.0, 0.0).astype(BF16))
    same = iota((TILE, LANES), 0) == (iota((TILE, LANES), 1) & (TILE - 1))
    same = jnp.where(same, 1.0, 0.0)
    parts = []
    for c in range(0, columns, LANES):
        part = jnp.broadcast_to(wide[:, None, c : c + LANES], (nblocks, TILE, LANES)) * same[None]
        parts.append(part.reshape(nblocks * TILE, LANES).astype(BF16))
    return jnp.concatenate(parts, axis=1)


def pieces(ref, u, nblocks, span):
    tiles = [
        jnp.concatenate(
            [ref[b * span + v * TILE : b * span + (v + 1) * TILE, :] for b in range(nblocks)], axis=0
        )
        for v in (u, u + 1)
    ]
    return jnp.concatenate(tiles, axis=1)


def prepare_kernel(chunks, chunk, nblocks, nbal, zones, rates, table, conc, *refs):
    span, width = BLK // chunks, LANES // chunks
    if chunk == 0:
        owners, factor, kept, keys, bases, value = refs
    else:
        factor, kept, value = refs

    decay = jnp.exp(-rates[...])
    lane = iota((span, LANES), 1)
    group = lax.shift_right_logical(lane, ZONES.bit_length() - 1)
    rows = []
    for j in range(chunks):
        turn = (j - chunk) % chunks * width
        moved = pltpu.roll(decay, turn, 1) if turn else decay
        rows.append(jnp.where(lax.shift_right_logical(iota(moved.shape, 1), width.bit_length() - 1) == j, moved, 0.0))
    if chunks * ZONES < LANES:
        rows.append(jnp.zeros((LANES - chunks * ZONES, LANES), F32))
    spread = jnp.concatenate(rows, axis=0)
    high = spread.astype(BF16)
    low = (spread - high.astype(F32)).astype(BF16)
    both = jnp.concatenate([high, low], axis=0)
    upright = dot_first(zones[...].astype(F32).astype(BF16), eye(nblocks))
    for b in range(nblocks):
        column = jnp.broadcast_to(upright[:, b : b + 1], (BLK, LANES))
        picked = column[:span]
        for j in range(1, chunks):
            picked = jnp.where(group == j, column[j * span : (j + 1) * span], picked)
        own = (picked == (lane - group * ZONES).astype(F32)) & (group < chunks)
        own = jnp.where(own, 1.0, 0.0).astype(BF16)
        factor[b] = dot(jnp.concatenate([own, own], axis=1), both)

    if chunk == 0:
        before = jnp.where(iota((BLK, LANES), 0) < iota((BLK, LANES), 1), 1.0, 0.0).astype(BF16)
        above = jnp.where(iota((nblocks, nblocks), 1) < iota((nblocks, nblocks), 0), 1.0, 0.0)
        windows = jnp.zeros((nblocks, LANES), F32)
        slot_lane = iota((nblocks, LANES), 1)
        relative = jnp.bitwise_xor(owners[...], lax.axis_index("bal"))
        step = TILE * chunks
        for k in range(nbal):
            mine = relative == k
            narrow = jnp.where(mine, 1.0, 0.0).astype(BF16)
            rank = dot(narrow, before)
            start = jnp.sum(dot(above.astype(BF16), narrow), axis=1, keepdims=True)
            window = jnp.floor(start * (1.0 / step))
            keys[k] = jnp.where(mine, rank + (start - window * step), -1.0)
            windows = jnp.where(slot_lane == k, window * TILE, windows)
        bases[...] = windows.astype(jnp.int32)

    coupling = table[...]
    kron = couple(coupling, 0, nblocks, nblocks)
    lane = iota((nblocks, LANES), 1)
    inner = jnp.sum(jnp.where(lane < nblocks, coupling, 0.0), axis=1, keepdims=True)
    keep = tall(1.0 - inner, TILE)
    for b in range(nblocks):
        rows = [conc[b * BLK + j * span : b * BLK + (j + 1) * span, :] for j in range(chunks)]
        value[b * span : (b + 1) * span, :] = regroup(rows, chunk, chunks)
    for u in range(0, span // TILE, 2):
        whole = pieces(value, u, nblocks, span)
        high = whole.astype(BF16)
        low = (whole - high.astype(F32)).astype(BF16)
        total = dot(kron, high) + dot(kron, low)
        for v in range(2):
            side = slice(v * LANES, (v + 1) * LANES)
            part = total[:, side] + keep * whole[:, side]
            for b in range(nblocks):
                kept[b, (u + v) * TILE : (u + v + 1) * TILE, :] = part[b * TILE : (b + 1) * TILE]


def mix_kernel(chunks, chunk, nblocks, nbal, bases, left, right, table, high, kept, factor, keys, *refs):
    span, width = BLK // chunks, LANES // chunks
    rows = nblocks * span
    start, slots = refs[0], refs[1:nbal]
    buffer, places, sem = refs[-3:]
    copy = pltpu.make_async_copy(bases, places, sem)
    copy.start()
    lane = iota((nblocks, LANES), 1)
    coupling = table[...]
    if chunk == 0:
        from_left = left[rows : rows + nblocks, :].astype(F32)
        from_right = right[rows : rows + nblocks, :].astype(F32)
        coupling = coupling + jnp.where((lane >= nblocks) & (lane < 2 * nblocks), from_left, 0.0)
        coupling = coupling + jnp.where((lane >= 2 * nblocks) & (lane < 3 * nblocks), from_right, 0.0)
        refs[nbal][...] = coupling
    outer = jnp.sum(jnp.where(lane < nblocks, 0.0, coupling), axis=1, keepdims=True)
    outer = tall(outer, TILE)
    kron = couple(coupling, nblocks, 2 * nblocks, nblocks)
    edge = nblocks * TILE

    for u in range(0, span // TILE, 2):
        total = dot(kron[:, :edge], pieces(left, u, nblocks, span))
        total = total + dot(kron[:, edge:], pieces(right, u, nblocks, span))
        for v in range(2):
            at = slice((u + v) * TILE, (u + v + 1) * TILE)
            for b in range(nblocks):
                mine = high[b * span + (u + v) * TILE : b * span + (u + v + 1) * TILE, :].astype(F32)
                tile = slice(b * TILE, (b + 1) * TILE)
                mixed = total[tile, v * LANES : (v + 1) * LANES] + kept[b, at, :]
                mixed = mixed - outer[tile] * mine
                start[b, at, :] = (mixed * factor[b, at, :]).astype(BF16)

    reach = span + TILE
    depth = slots[0].shape[0]
    buffer[...] = jnp.zeros(buffer.shape, BF16)
    line = iota((reach, LANES), 0)
    marks = [
        ((line >> SHIFT) * (TILE * chunks) + jj * TILE + (line & (TILE - 1))).astype(F32)
        for jj in range(chunks)
    ]
    group = lax.shift_right_logical(iota((reach, LANES), 1), width.bit_length() - 1)
    copy.wait()
    for b in range(nblocks):
        select = []
        for k in range(1, nbal):
            key = jnp.broadcast_to(keys[k, b : b + 1, :], (reach, LANES))
            select += [jnp.where(key == m, 1.0, 0.0).astype(BF16) for m in marks]
        spread = [regroup([start[b]] * chunks, j, chunks) for j in range(chunks)]
        placed = dot(jnp.concatenate(select, axis=0), jnp.concatenate(spread, axis=0))
        for k in range(1, nbal):
            first = (k - 1) * chunks * reach
            window = placed[first : first + reach]
            for jj in range(1, chunks):
                other = placed[first + jj * reach : first + (jj + 1) * reach]
                window = jnp.where(group == jj, other, window)
            window = window.astype(BF16)
            at = pl.multiple_of(jnp.minimum(places[b, k], depth), TILE)
            buffer[k - 1, pl.ds(at, TILE), :] = buffer[k - 1, pl.ds(at, TILE), :] + window[:TILE]
            buffer[k - 1, pl.ds(at + TILE, span), :] = window[TILE:]
    for k in range(1, nbal):
        slots[k - 1][...] = buffer[k - 1, :depth, :]


def chemistry(state, reaction):
    quarter = (reaction[...].astype(F32) * 0.25).astype(BF16)
    rows = state.shape[0] // TILES
    for _ in range(SUBSTEPS):
        for t in range(TILES):
            current = state[t * rows : (t + 1) * rows, :]
            tendency = dot(current.astype(BF16), quarter)
            state[t * rows : (t + 1) * rows, :] = current + jnp.tanh(tendency)


def own_kernel(chunks, nblocks, nbal, bases, reaction, keys, *refs):
    starts, out, slots, lates = refs[:chunks], refs[chunks], refs[chunks + 1], refs[chunks + 2 : -6]
    state, done, mine, others, places, sems = refs[-6:]
    copy = pltpu.make_async_copy(bases, places, sems.at[1])
    copy.start()
    span, capacity, late = BLK // chunks, slots.shape[0], lates[0].shape[0]
    for b in range(nblocks):
        for j in range(chunks):
            first = b * BLK + j * span
            rows = regroup([starts[c][b] for c in range(chunks)], j, chunks)
            state[first : first + span, :] = rows.astype(F32) * 4.0
    chemistry(state, reaction)
    done[...] = (state[...] * 0.25).astype(BF16)
    result = pltpu.make_async_copy(done, out, sems.at[0])
    result.start()
    edge = TILE * chunks
    reach = BLK + edge
    mine[...] = jnp.zeros(mine.shape, BF16)
    others[...] = jnp.zeros(others.shape, BF16)
    mark = iota((reach, LANES), 0).astype(F32)
    copy.wait()
    for b in range(nblocks):
        select = []
        for k in range(nbal):
            key = jnp.broadcast_to(keys[k, b : b + 1, :], (reach, LANES))
            select.append(jnp.where(key == mark, 1.0, 0.0).astype(BF16))
        placed = dot(jnp.concatenate(select, axis=0), done[b * BLK : (b + 1) * BLK, :]).astype(BF16)
        for k in range(nbal):
            at = places[b, k] * chunks
            target = mine
            if k:
                at = jnp.maximum(at - (capacity - late - reach), 0)
                target = others.at[k - 1]
            at = pl.multiple_of(at, TILE)
            window = placed[k * reach : (k + 1) * reach]
            target[pl.ds(at, edge), :] = target[pl.ds(at, edge), :] + window[:edge]
            target[pl.ds(at + edge, BLK), :] = window[edge:]
    slots[...] = mine[:capacity, :]
    for k in range(1, nbal):
        lates[k - 1][...] = others[k - 1, reach : reach + late, :]
    result.wait()


def slot_kernel(chunks, nbal, reaction, mine, *refs):
    parts = refs[: (nbal - 1) * chunks]
    out, state, result, sems = refs[-4:]
    depth = parts[0].shape[0]
    early = depth * chunks
    own = pltpu.make_async_copy(mine, out.at[lax.axis_index("bal")], sems.at[nbal - 1])
    own.start()
    for k in range(1, nbal):
        mine = parts[(k - 1) * chunks : k * chunks]
        for jj in range(chunks):
            first = (k - 1) * early + jj * depth
            rows = regroup([part[...] for part in mine], jj, chunks)
            state[first : first + depth, :] = rows.astype(F32) * 4.0
    chemistry(state, reaction)
    copies = []
    for k in range(1, nbal):
        for jj in range(chunks):
            first = (k - 1) * early + jj * depth
            done = (state[first : first + depth, :] * 0.25).astype(BF16)
            result[k - 1, :, jj] = done.reshape(depth // TILE, TILE, LANES)
        place = jnp.bitwise_xor(lax.axis_index("bal"), k)
        copies.append(
            pltpu.make_async_copy(
                result.at[k - 1].reshape(early, LANES),
                out.at[place, pl.ds(0, early)],
                sems.at[k - 1],
            )
        )
        copies[-1].start()
    own.wait()
    for copy in copies:
        copy.wait()


def late_kernel(nbal, *refs):
    lates, out, sems = refs[: nbal - 1], refs[-2], refs[-1]
    late = lates[0].shape[0]
    copies = []
    for k in range(1, nbal):
        place = jnp.bitwise_xor(lax.axis_index("bal"), k)
        target = out.at[place, pl.ds(out.shape[1] - late, late)]
        copies.append(pltpu.make_async_copy(lates[k - 1], target, sems.at[k - 1]))
        copies[-1].start()
    for copy in copies:
        copy.wait()


def step(conc, neighbours, counts, weights, zones, owners, rate_table, reaction):
    rows, width = conc.shape
    nblocks = rows // BLK
    nlon, nbal = lax.axis_size("lon"), lax.axis_size("bal")
    chunks = CHUNKS
    span = BLK // chunks
    capacity = 2 * rows // nbal
    late = capacity * LATE // 16
    depth = (capacity - late) // chunks

    shape = jax.ShapeDtypeStruct
    zones, owners = zones.reshape(nblocks, BLK), owners.reshape(nblocks, BLK)
    blocked = shape((nblocks, span, LANES), F32)

    def call(body, **kw):
        params = pltpu.CompilerParams(vmem_limit_bytes=16 << 20)
        return pl.pallas_call(body, compiler_params=params, **kw)

    def in_hbm(array):
        return pltpu.with_memory_space_constraint(array, pltpu.HBM)

    ahead = [(i, (i + 1) % nlon) for i in range(nlon)]
    back = [((i + 1) % nlon, i) for i in range(nlon)]
    lists = (neighbours.T, counts.reshape(1, nblocks), weights.T)
    msgs, lefts, rights, table = [], [], [], None
    for c in range(chunks):
        first = c == 0
        length = nblocks * span + (nblocks if first else 0)
        outs = call(
            functools.partial(pack_kernel, chunks, c, nblocks),
            out_shape=[shape((length, LANES), BF16)]
            + [shape((nblocks, LANES), F32), shape((rows, LANES), F32)] * first,
            in_specs=[HBM] * 4 if first else [VMEM],
            out_specs=[VMEM] * (1 + 2 * first),
            scratch_shapes=[pltpu.VMEM(a.shape, jnp.int32) for a in lists if first]
            + [pltpu.SemaphoreType.DMA((LOADS + 3,))] * first,
        )(*((in_hbm(conc), *map(in_hbm, lists)) if first else (stage,)))
        if first:
            table, stage = outs[1:]
        msgs.append(outs[0])
        lefts.append(lax.ppermute(outs[0], "lon", ahead))
        rights.append(lax.ppermute(outs[0], "lon", back))

    factors, kepts, keys, bases = [], [], None, None
    for c in range(chunks):
        first = c == 0
        outs = call(
            functools.partial(prepare_kernel, chunks, c, nblocks, nbal),
            out_shape=[blocked, blocked]
            + [shape((nbal, nblocks, LANES), F32), shape((nblocks, LANES), jnp.int32)] * first,
            in_specs=[VMEM] * (4 + first),
            out_specs=[VMEM] * (2 + 2 * first),
            scratch_shapes=[pltpu.VMEM((nblocks * span, LANES), F32)],
        )(zones, rate_table, table, stage, *([owners] if first else []))
        factors.append(outs[0])
        kepts.append(outs[1])
        if first:
            keys, bases = outs[2:]

    starts, received = [], [[None] * chunks for _ in range(nbal)]
    for c in range(chunks):
        first = c == 0
        outs = call(
            functools.partial(mix_kernel, chunks, c, nblocks, nbal),
            out_shape=[shape((nblocks, span, LANES), BF16)]
            + [shape((depth, LANES), BF16)] * (nbal - 1)
            + [shape((nblocks, LANES), F32)] * first,
            in_specs=[VMEM] * 8,
            out_specs=[VMEM] * (nbal + first),
            scratch_shapes=[
                pltpu.VMEM((nbal - 1, depth + span + TILE, LANES), BF16),
                pltpu.SMEM(bases.shape, jnp.int32),
                pltpu.SemaphoreType.DMA,
            ],
        )(bases, lefts[c], rights[c], table, msgs[c], kepts[c], factors[c], keys)
        starts.append(outs[0])
        if first:
            table = outs[nbal]
        for k in range(1, nbal):
            received[k][c] = lax.ppermute(outs[k], "bal", [(i, i ^ k) for i in range(nbal)])

    slots = shape((nbal, capacity, LANES), BF16)
    reach = BLK + TILE * chunks
    conc_out, mine, *lates = call(
        functools.partial(own_kernel, chunks, nblocks, nbal),
        out_shape=[shape((rows, LANES), BF16), shape((capacity, LANES), BF16)]
            + [shape((late, LANES), BF16)] * (nbal - 1),
        in_specs=[VMEM] * (3 + chunks),
        out_specs=[ANY] + [VMEM] * nbal,
        scratch_shapes=[
            pltpu.VMEM((rows, LANES), F32),
            pltpu.VMEM((rows, LANES), BF16),
            pltpu.VMEM((capacity + reach, LANES), BF16),
            pltpu.VMEM((nbal - 1, late + 2 * reach, LANES), BF16),
            pltpu.SMEM(bases.shape, jnp.int32),
            pltpu.SemaphoreType.DMA((2,)),
        ],
    )(bases, reaction, keys, *starts)
    for k in range(1, nbal):
        moved = lax.ppermute(lates[k - 1], "bal", [(i, i ^ k) for i in range(nbal)])
        lates[k - 1] = moved
    chem = call(
        functools.partial(slot_kernel, chunks, nbal),
        out_shape=slots,
        in_specs=[VMEM] * (2 + chunks * (nbal - 1)),
        out_specs=ANY,
        scratch_shapes=[
            pltpu.VMEM(((nbal - 1) * (capacity - late), LANES), F32),
            pltpu.VMEM((nbal - 1, depth // TILE, chunks, TILE, LANES), BF16),
            pltpu.SemaphoreType.DMA((nbal,)),
        ],
    )(reaction, mine, *[part for group in received[1:] for part in group])
    chem = call(
        functools.partial(late_kernel, nbal),
        out_shape=slots,
        in_specs=[VMEM] * (nbal - 1) + [ANY],
        out_specs=ANY,
        scratch_shapes=[pltpu.SemaphoreType.DMA((nbal - 1,))],
        input_output_aliases={nbal - 1: 0},
    )(*lates, chem)
    return conc_out, chem.reshape(nbal * capacity, width)


def solution(mesh):
    in_specs = (
        P(("lon", "bal"), None),
        P(("lon", "bal"), None),
        P(("lon", "bal")),
        P(("lon", "bal"), None),
        P(("lon", "bal")),
        P(("lon", "bal"), None),
        P(),
        P(),
    )
    out_specs = (P(("lon", "bal"), None), P(("lon", "bal"), None))
    return jax.shard_map(step, mesh=mesh, in_specs=in_specs, out_specs=out_specs, check_vma=False)
```

```python
import functools

import jax
import jax.numpy as jnp
from jax import lax
from jax.experimental import pallas as pl
from jax.experimental.pallas import tpu as pltpu
from jax.sharding import PartitionSpec as P


BLK = 128
LANES = 128
TILE = 16
SHIFT = 4
ZONES = 32
SUBSTEPS = 12
CHUNKS = 2
LOADS = 4
TILES = 4
LATE = 6

F32 = jnp.float32
BF16 = jnp.bfloat16
VMEM = pl.BlockSpec(memory_space=pltpu.VMEM)
ANY = pl.BlockSpec(memory_space=pl.ANY)
HBM = pl.BlockSpec(memory_space=pltpu.HBM)


def iota(shape, axis):
    return lax.broadcasted_iota(jnp.int32, shape, axis)


def dot(a, b):
    return jnp.dot(a, b, preferred_element_type=F32)


def dot_first(a, b):
    return lax.dot_general(a, b, (((0,), (0,)), ((), ())), preferred_element_type=F32)


def eye(rows, shift=0):
    shape = (rows, LANES)
    return jnp.where(iota(shape, 0) + shift == iota(shape, 1), 1.0, 0.0).astype(BF16)


def regroup(parts, source, chunks):
    width = LANES // chunks
    group = lax.shift_right_logical(iota(parts[0].shape, 1), width.bit_length() - 1)
    out = None
    for place in range(chunks):
        moved = parts[place]
        turn = (place - source) % chunks * width
        if turn:
            moved = pltpu.roll(moved, turn, 1)
        out = moved if out is None else jnp.where(group == place, moved, out)
    return out


def load_all(source, target, sems):
    rows = target.shape[0] // LOADS
    copies = [
        pltpu.make_async_copy(
            source.at[pl.ds(i * rows, rows)], target.at[pl.ds(i * rows, rows)], sems.at[i]
        )
        for i in range(LOADS)
    ]
    for copy in copies:
        copy.start()
    return copies


def pack_kernel(chunks, chunk, nblocks, conc, *refs):
    span = BLK // chunks
    loads, stage = [], conc
    if chunk == 0:
        lists, msg, table, stage, held, sems = refs[:3], *refs[3:6], refs[6:9], refs[9]
        small = [
            pltpu.make_async_copy(source, target, sems.at[LOADS + i])
            for i, (source, target) in enumerate(zip(lists, held))
        ]
        for copy in small:
            copy.start()
        loads = load_all(conc, stage, sems)
        for copy in small:
            copy.wait()
        neighbours, counts, weights = held
        nlon, nbal = lax.axis_size("lon"), lax.axis_size("bal")
        me = lax.axis_index("lon") * nbal + lax.axis_index("bal")
        column = iota((3 * nblocks, nblocks), 0)
        pairs = jnp.zeros((3 * nblocks, nblocks), jnp.int32)
        for k in range(neighbours.shape[0]):
            target = neighbours[k : k + 1, :]
            device = lax.div(target, nblocks)
            apart = device - me
            right = (apart == nbal) | (apart == nbal - nlon * nbal)
            place = jnp.where(apart == 0, 0, jnp.where(right, 2 * nblocks, nblocks))
            place = place + target - device * nblocks
            weight = jnp.where(k < counts[...], weights[k : k + 1, :], 0)
            pairs = pairs + jnp.where(column == place, weight, 0)
        pairs = jnp.where(column == iota(column.shape, 1), 0, pairs)
        pairs = (pairs.astype(F32) * (1.0 / BLK)).astype(BF16)
        table[...] = dot_first(pairs, eye(3 * nblocks)) + dot(pairs[:nblocks], eye(nblocks))
        carried = dot(pairs[2 * nblocks :], eye(nblocks, nblocks))
        carried = carried + dot(pairs[nblocks : 2 * nblocks], eye(nblocks, 2 * nblocks))
        msg[nblocks * span :, :] = carried.astype(BF16)
    else:
        (msg,) = refs
    each = nblocks // LOADS
    for b in range(nblocks):
        if loads and b % each == 0:
            loads[b // each].wait()
        rows = [stage[b * BLK + j * span : b * BLK + (j + 1) * span, :] for j in range(chunks)]
        rows = [row.astype(BF16) for row in rows]
        msg[b * span : (b + 1) * span, :] = regroup(rows, chunk, chunks)


def tall(value, rows):
    nblocks = value.shape[0]
    value = jnp.broadcast_to(value, (nblocks, LANES))
    wide = jnp.broadcast_to(value[:, None, :], (nblocks, rows, LANES))
    return wide.reshape(nblocks * rows, LANES)


def couple(table, first, blocks, nblocks):
    same = iota((TILE, LANES), 0) == (iota((TILE, LANES), 1) & (TILE - 1))
    same = jnp.where(same, 1.0, 0.0)
    group = iota((nblocks, LANES), 1) >> SHIFT
    parts = []
    for h in range(first, first + blocks, LANES // TILE):
        wide = None
        for j in range(LANES // TILE):
            column = jnp.broadcast_to(table[:, h + j : h + j + 1], (nblocks, LANES))
            wide = column if wide is None else jnp.where(group == j, column, wide)
        part = jnp.broadcast_to(wide[:, None, :], (nblocks, TILE, LANES)) * same[None]
        parts.append(part.reshape(nblocks * TILE, LANES).astype(BF16))
    return jnp.concatenate(parts, axis=1)


def pieces(ref, u, nblocks, span):
    tiles = [
        jnp.concatenate(
            [ref[b * span + v * TILE : b * span + (v + 1) * TILE, :] for b in range(nblocks)], axis=0
        )
        for v in (u, u + 1)
    ]
    return jnp.concatenate(tiles, axis=1)


def prepare_kernel(chunks, chunk, nblocks, nbal, zones, rates, table, conc, *refs):
    span, width = BLK // chunks, LANES // chunks
    if chunk == 0:
        owners, factor, kept, keys, bases, value = refs
    else:
        factor, kept, value = refs

    decay = jnp.exp(-rates[...])
    lane = iota((span, LANES), 1)
    group = lax.shift_right_logical(lane, ZONES.bit_length() - 1)
    rows = []
    for j in range(chunks):
        turn = (j - chunk) % chunks * width
        moved = pltpu.roll(decay, turn, 1) if turn else decay
        rows.append(jnp.where(lax.shift_right_logical(iota(moved.shape, 1), width.bit_length() - 1) == j, moved, 0.0))
    if chunks * ZONES < LANES:
        rows.append(jnp.zeros((LANES - chunks * ZONES, LANES), F32))
    spread = jnp.concatenate(rows, axis=0)
    high = spread.astype(BF16)
    low = (spread - high.astype(F32)).astype(BF16)
    both = jnp.concatenate([high, low], axis=0)
    upright = dot_first(zones[...].astype(F32).astype(BF16), eye(nblocks))
    for b in range(nblocks):
        column = jnp.broadcast_to(upright[:, b : b + 1], (BLK, LANES))
        picked = column[:span]
        for j in range(1, chunks):
            picked = jnp.where(group == j, column[j * span : (j + 1) * span], picked)
        own = (picked == (lane - group * ZONES).astype(F32)) & (group < chunks)
        own = jnp.where(own, 1.0, 0.0).astype(BF16)
        factor[b] = dot(jnp.concatenate([own, own], axis=1), both)

    if chunk == 0:
        before = jnp.where(iota((BLK, LANES), 0) < iota((BLK, LANES), 1), 1.0, 0.0).astype(BF16)
        above = jnp.where(iota((nblocks, nblocks), 1) < iota((nblocks, nblocks), 0), 1.0, 0.0)
        windows = jnp.zeros((nblocks, LANES), F32)
        slot_lane = iota((nblocks, LANES), 1)
        relative = jnp.bitwise_xor(owners[...], lax.axis_index("bal"))
        step = TILE * chunks
        for k in range(nbal):
            mine = relative == k
            narrow = jnp.where(mine, 1.0, 0.0).astype(BF16)
            rank = dot(narrow, before)
            start = jnp.sum(dot(above.astype(BF16), narrow), axis=1, keepdims=True)
            window = jnp.floor(start * (1.0 / step))
            keys[k] = jnp.where(mine, rank + (start - window * step), -1.0)
            windows = jnp.where(slot_lane == k, window * TILE, windows)
        bases[...] = windows.astype(jnp.int32)

    coupling = table[...]
    kron = couple(coupling, 0, nblocks, nblocks)
    lane = iota((nblocks, LANES), 1)
    inner = jnp.sum(jnp.where(lane < nblocks, coupling, 0.0), axis=1, keepdims=True)
    keep = tall(1.0 - inner, TILE)
    for b in range(nblocks):
        rows = [conc[b * BLK + j * span : b * BLK + (j + 1) * span, :] for j in range(chunks)]
        value[b * span : (b + 1) * span, :] = regroup(rows, chunk, chunks)
    for u in range(0, span // TILE, 2):
        whole = pieces(value, u, nblocks, span)
        high = whole.astype(BF16)
        low = (whole - high.astype(F32)).astype(BF16)
        total = dot(kron, high) + dot(kron, low)
        for v in range(2):
            side = slice(v * LANES, (v + 1) * LANES)
            part = total[:, side] + keep * whole[:, side]
            for b in range(nblocks):
                kept[b, (u + v) * TILE : (u + v + 1) * TILE, :] = part[b * TILE : (b + 1) * TILE]


def mix_kernel(chunks, chunk, nblocks, nbal, bases, left, right, table, high, kept, factor, keys, *refs):
    span, width = BLK // chunks, LANES // chunks
    rows = nblocks * span
    start, slots = refs[0], refs[1:nbal]
    buffer, places, sem = refs[-3:]
    copy = pltpu.make_async_copy(bases, places, sem)
    copy.start()
    lane = iota((nblocks, LANES), 1)
    coupling = table[...]
    if chunk == 0:
        from_left = left[rows : rows + nblocks, :].astype(F32)
        from_right = right[rows : rows + nblocks, :].astype(F32)
        coupling = coupling + jnp.where((lane >= nblocks) & (lane < 2 * nblocks), from_left, 0.0)
        coupling = coupling + jnp.where((lane >= 2 * nblocks) & (lane < 3 * nblocks), from_right, 0.0)
        refs[nbal][...] = coupling
    outer = jnp.sum(jnp.where(lane < nblocks, 0.0, coupling), axis=1, keepdims=True)
    outer = tall(outer, TILE)
    kron = couple(coupling, nblocks, 2 * nblocks, nblocks)
    edge = nblocks * TILE

    for u in range(0, span // TILE, 2):
        total = dot(kron[:, :edge], pieces(left, u, nblocks, span))
        total = total + dot(kron[:, edge:], pieces(right, u, nblocks, span))
        for v in range(2):
            at = slice((u + v) * TILE, (u + v + 1) * TILE)
            for b in range(nblocks):
                mine = high[b * span + (u + v) * TILE : b * span + (u + v + 1) * TILE, :].astype(F32)
                tile = slice(b * TILE, (b + 1) * TILE)
                mixed = total[tile, v * LANES : (v + 1) * LANES] + kept[b, at, :]
                mixed = mixed - outer[tile] * mine
                start[b, at, :] = (mixed * factor[b, at, :]).astype(BF16)

    reach = span + TILE
    depth = slots[0].shape[0]
    buffer[...] = jnp.zeros(buffer.shape, BF16)
    line = iota((reach, LANES), 0)
    marks = [
        ((line >> SHIFT) * (TILE * chunks) + jj * TILE + (line & (TILE - 1))).astype(F32)
        for jj in range(chunks)
    ]
    group = lax.shift_right_logical(iota((reach, LANES), 1), width.bit_length() - 1)
    copy.wait()
    for b in range(nblocks):
        select = []
        for k in range(1, nbal):
            key = jnp.broadcast_to(keys[k, b : b + 1, :], (reach, LANES))
            select += [jnp.where(key == m, 1.0, 0.0).astype(BF16) for m in marks]
        spread = [regroup([start[b]] * chunks, j, chunks) for j in range(chunks)]
        placed = dot(jnp.concatenate(select, axis=0), jnp.concatenate(spread, axis=0))
        for k in range(1, nbal):
            first = (k - 1) * chunks * reach
            window = placed[first : first + reach]
            for jj in range(1, chunks):
                other = placed[first + jj * reach : first + (jj + 1) * reach]
                window = jnp.where(group == jj, other, window)
            window = window.astype(BF16)
            at = pl.multiple_of(jnp.minimum(places[b, k], depth), TILE)
            buffer[k - 1, pl.ds(at, TILE), :] = buffer[k - 1, pl.ds(at, TILE), :] + window[:TILE]
            buffer[k - 1, pl.ds(at + TILE, span), :] = window[TILE:]
    for k in range(1, nbal):
        slots[k - 1][...] = buffer[k - 1, :depth, :]


def chemistry(state, reaction):
    quarter = (reaction[...].astype(F32) * 0.25).astype(BF16)
    rows = state.shape[0] // TILES
    for _ in range(SUBSTEPS):
        for t in range(TILES):
            current = state[t * rows : (t + 1) * rows, :]
            tendency = dot(current.astype(BF16), quarter)
            state[t * rows : (t + 1) * rows, :] = current + jnp.tanh(tendency)


def own_kernel(chunks, nblocks, nbal, bases, reaction, keys, *refs):
    starts, out, slots, lates = refs[:chunks], refs[chunks], refs[chunks + 1], refs[chunks + 2 : -6]
    state, done, mine, others, places, sems = refs[-6:]
    copy = pltpu.make_async_copy(bases, places, sems.at[1])
    copy.start()
    span, capacity, late = BLK // chunks, slots.shape[0], lates[0].shape[0]
    for b in range(nblocks):
        for j in range(chunks):
            first = b * BLK + j * span
            rows = regroup([starts[c][b] for c in range(chunks)], j, chunks)
            state[first : first + span, :] = rows.astype(F32) * 4.0
    mine[...] = jnp.zeros(mine.shape, BF16)
    others[...] = jnp.zeros(others.shape, BF16)
    chemistry(state, reaction)
    done[...] = (state[...] * 0.25).astype(BF16)
    result = pltpu.make_async_copy(done, out, sems.at[0])
    result.start()
    edge = TILE * chunks
    reach = BLK + edge
    mark = iota((reach, LANES), 0).astype(F32)
    copy.wait()
    for b in range(nblocks):
        select = []
        for k in range(nbal):
            key = jnp.broadcast_to(keys[k, b : b + 1, :], (reach, LANES))
            select.append(jnp.where(key == mark, 1.0, 0.0).astype(BF16))
        placed = dot(jnp.concatenate(select, axis=0), done[b * BLK : (b + 1) * BLK, :]).astype(BF16)
        for k in range(nbal):
            at = places[b, k] * chunks
            target = mine
            if k:
                at = jnp.maximum(at - (capacity - late - reach), 0)
                target = others.at[k - 1]
            at = pl.multiple_of(at, TILE)
            window = placed[k * reach : (k + 1) * reach]
            target[pl.ds(at, edge), :] = target[pl.ds(at, edge), :] + window[:edge]
            target[pl.ds(at + edge, BLK), :] = window[edge:]
    slots[...] = mine[:capacity, :]
    for k in range(1, nbal):
        lates[k - 1][...] = others[k - 1, reach : reach + late, :]
    result.wait()


def slot_kernel(chunks, nbal, reaction, mine, *refs):
    parts = refs[: (nbal - 1) * chunks]
    out, state, result, sems = refs[-4:]
    depth = parts[0].shape[0]
    early = depth * chunks
    own = pltpu.make_async_copy(mine, out.at[lax.axis_index("bal")], sems.at[nbal - 1])
    own.start()
    for k in range(1, nbal):
        mine = parts[(k - 1) * chunks : k * chunks]
        for jj in range(chunks):
            first = (k - 1) * early + jj * depth
            rows = regroup([part[...] for part in mine], jj, chunks)
            state[first : first + depth, :] = rows.astype(F32) * 4.0
    chemistry(state, reaction)
    copies = []
    for k in range(1, nbal):
        for jj in range(chunks):
            first = (k - 1) * early + jj * depth
            done = (state[first : first + depth, :] * 0.25).astype(BF16)
            result[k - 1, :, jj] = done.reshape(depth // TILE, TILE, LANES)
        place = jnp.bitwise_xor(lax.axis_index("bal"), k)
        copies.append(
            pltpu.make_async_copy(
                result.at[k - 1].reshape(early, LANES),
                out.at[place, pl.ds(0, early)],
                sems.at[k - 1],
            )
        )
        copies[-1].start()
    own.wait()
    for copy in copies:
        copy.wait()


def late_kernel(nbal, *refs):
    lates, out, sems = refs[: nbal - 1], refs[-2], refs[-1]
    late = lates[0].shape[0]
    copies = []
    for k in range(1, nbal):
        place = jnp.bitwise_xor(lax.axis_index("bal"), k)
        target = out.at[place, pl.ds(out.shape[1] - late, late)]
        copies.append(pltpu.make_async_copy(lates[k - 1], target, sems.at[k - 1]))
        copies[-1].start()
    for copy in copies:
        copy.wait()


def step(conc, neighbours, counts, weights, zones, owners, rate_table, reaction):
    rows, width = conc.shape
    nblocks = rows // BLK
    nlon, nbal = lax.axis_size("lon"), lax.axis_size("bal")
    chunks = CHUNKS
    span = BLK // chunks
    capacity = 2 * rows // nbal
    late = capacity * LATE // 16
    depth = (capacity - late) // chunks

    shape = jax.ShapeDtypeStruct
    zones, owners = zones.reshape(nblocks, BLK), owners.reshape(nblocks, BLK)
    blocked = shape((nblocks, span, LANES), F32)

    def call(body, **kw):
        params = pltpu.CompilerParams(vmem_limit_bytes=16 << 20)
        return pl.pallas_call(body, compiler_params=params, **kw)

    def in_hbm(array):
        return pltpu.with_memory_space_constraint(array, pltpu.HBM)

    ahead = [(i, (i + 1) % nlon) for i in range(nlon)]
    back = [((i + 1) % nlon, i) for i in range(nlon)]
    lists = (neighbours.T, counts.reshape(1, nblocks), weights.T)
    msgs, lefts, rights, table = [], [], [], None
    for c in range(chunks):
        first = c == 0
        length = nblocks * span + (nblocks if first else 0)
        outs = call(
            functools.partial(pack_kernel, chunks, c, nblocks),
            out_shape=[shape((length, LANES), BF16)]
            + [shape((nblocks, LANES), F32), shape((rows, LANES), F32)] * first,
            in_specs=[HBM] * 4 if first else [VMEM],
            out_specs=[VMEM] * (1 + 2 * first),
            scratch_shapes=[pltpu.VMEM(a.shape, jnp.int32) for a in lists if first]
            + [pltpu.SemaphoreType.DMA((LOADS + 3,))] * first,
        )(*((in_hbm(conc), *map(in_hbm, lists)) if first else (stage,)))
        if first:
            table, stage = outs[1:]
        msgs.append(outs[0])
        lefts.append(lax.ppermute(outs[0], "lon", ahead))
        rights.append(lax.ppermute(outs[0], "lon", back))

    factors, kepts, keys, bases = [], [], None, None
    for c in range(chunks):
        first = c == 0
        outs = call(
            functools.partial(prepare_kernel, chunks, c, nblocks, nbal),
            out_shape=[blocked, blocked]
            + [shape((nbal, nblocks, LANES), F32), shape((nblocks, LANES), jnp.int32)] * first,
            in_specs=[VMEM] * (4 + first),
            out_specs=[VMEM] * (2 + 2 * first),
            scratch_shapes=[pltpu.VMEM((nblocks * span, LANES), F32)],
        )(zones, rate_table, table, stage, *([owners] if first else []))
        factors.append(outs[0])
        kepts.append(outs[1])
        if first:
            keys, bases = outs[2:]

    starts, received = [], [[None] * chunks for _ in range(nbal)]
    for c in range(chunks):
        first = c == 0
        outs = call(
            functools.partial(mix_kernel, chunks, c, nblocks, nbal),
            out_shape=[shape((nblocks, span, LANES), BF16)]
            + [shape((depth, LANES), BF16)] * (nbal - 1)
            + [shape((nblocks, LANES), F32)] * first,
            in_specs=[VMEM] * 8,
            out_specs=[VMEM] * (nbal + first),
            scratch_shapes=[
                pltpu.VMEM((nbal - 1, depth + span + TILE, LANES), BF16),
                pltpu.SMEM(bases.shape, jnp.int32),
                pltpu.SemaphoreType.DMA,
            ],
        )(bases, lefts[c], rights[c], table, msgs[c], kepts[c], factors[c], keys)
        starts.append(outs[0])
        if first:
            table = outs[nbal]
        for k in range(1, nbal):
            received[k][c] = lax.ppermute(outs[k], "bal", [(i, i ^ k) for i in range(nbal)])

    slots = shape((nbal, capacity, LANES), BF16)
    reach = BLK + TILE * chunks
    conc_out, mine, *lates = call(
        functools.partial(own_kernel, chunks, nblocks, nbal),
        out_shape=[shape((rows, LANES), BF16), shape((capacity, LANES), BF16)]
            + [shape((late, LANES), BF16)] * (nbal - 1),
        in_specs=[VMEM] * (3 + chunks),
        out_specs=[ANY] + [VMEM] * nbal,
        scratch_shapes=[
            pltpu.VMEM((rows, LANES), F32),
            pltpu.VMEM((rows, LANES), BF16),
            pltpu.VMEM((capacity + reach, LANES), BF16),
            pltpu.VMEM((nbal - 1, late + 2 * reach, LANES), BF16),
            pltpu.SMEM(bases.shape, jnp.int32),
            pltpu.SemaphoreType.DMA((2,)),
        ],
    )(bases, reaction, keys, *starts)
    for k in range(1, nbal):
        moved = lax.ppermute(lates[k - 1], "bal", [(i, i ^ k) for i in range(nbal)])
        lates[k - 1] = moved
    chem = call(
        functools.partial(slot_kernel, chunks, nbal),
        out_shape=slots,
        in_specs=[VMEM] * (2 + chunks * (nbal - 1)),
        out_specs=ANY,
        scratch_shapes=[
            pltpu.VMEM(((nbal - 1) * (capacity - late), LANES), F32),
            pltpu.VMEM((nbal - 1, depth // TILE, chunks, TILE, LANES), BF16),
            pltpu.SemaphoreType.DMA((nbal,)),
        ],
    )(reaction, mine, *[part for group in received[1:] for part in group])
    chem = call(
        functools.partial(late_kernel, nbal),
        out_shape=slots,
        in_specs=[VMEM] * (nbal - 1) + [ANY],
        out_specs=ANY,
        scratch_shapes=[pltpu.SemaphoreType.DMA((nbal - 1,))],
        input_output_aliases={nbal - 1: 0},
    )(*lates, chem)
    return conc_out, chem.reshape(nbal * capacity, width)


def solution(mesh):
    in_specs = (
        P(("lon", "bal"), None),
        P(("lon", "bal"), None),
        P(("lon", "bal")),
        P(("lon", "bal"), None),
        P(("lon", "bal")),
        P(("lon", "bal"), None),
        P(),
        P(),
    )
    out_specs = (P(("lon", "bal"), None), P(("lon", "bal"), None))
    return jax.shard_map(step, mesh=mesh, in_specs=in_specs, out_specs=out_specs, check_vma=False)
```
